512 devices in a mesh: grp: 8 (over x, core), own: 64 (over z, y).
Axes of the slice: x: 4, y: 4, z: 16, core: 2. Of those that a mesh axis runs over, the one named last changes fastest.
Arguments:
- features: bfloat16 [131072, 128], P(('grp', 'own')), may hold values from -6 to 6
- scenario_ids: int32 [131072], P(('grp', 'own')), may hold values from 0 to 63, as said below
- labels: int32 [2, 131072], P(None, ('grp', 'own')), may hold values 0 or 1
- counts: int32 [64], replicated, may hold values from 400 to 39999
- scenario_weights: bfloat16 [64, 128, 4096], P('own'), may hold values from -0.5 to 0.5
- shared_weights: bfloat16 [128, 4096], replicated, may hold values from -0.5 to 0.5
- gate_weights: bfloat16 [128, 2], replicated, may hold values from -0.5 to 0.5
- tower_weights: bfloat16 [4096, 256], replicated, may hold values from -0.09375 to 0.09375
- tower_out: bfloat16 [256], replicated, may hold values from -0.5 to 0.5
Outputs:
- logits: float32 [2, 131072], P(None, ('grp', 'own'))
- scenario_grad: float32 [64, 128, 4096], P('own', 'grp')
The draws below stay inside these ranges and needn't reach their ends.
Inputs may be any that keep to these rules, and one draw needn't show every extreme that they name: `scenario_ids`: among the samples of one device each scenario occurs at most 8 times; in every group of 64 consecutive devices' samples some scenario occurs exactly 8 times on each of the devices.
All inputs are finite; a program needn't handle non-finite values. No bound on the sum of `labels` on one device may be relied on, other than what follows from the above.
Results may differ from the reference program's by a relative error of at most 0.0158.
The reference program's roundings to bfloat16 on the way count: a program that leaves them out, or rounds other values in their place, can miss the bound.
Values may be sent and summed in bfloat16 or wider, within the bound.
A program may use at most 64 MiB of HBM per device.

```python
import jax
import jax.numpy as jnp
from jax import lax

D = 128
E = 4096
TH = 128
TASKS = 2
TOK_DEV = 256
SCENARIOS = 64
CAP = 8
TOKENS = 131072


def draw_scenario_ids(key, part):
    blocks = TOKENS // TOK_DEV
    groups = blocks // SCENARIOS
    entries = SCENARIOS * CAP
    key_hot, key_level, key_jitter, key_order = jax.random.split(key, 4)
    hottest = jax.random.randint(key_hot, (groups,), 0, SCENARIOS)
    hottest_block = jnp.repeat(hottest, SCENARIOS)
    levels = jax.random.randint(key_level, (blocks, SCENARIOS), 0, 4)
    levels = jnp.where(jnp.arange(SCENARIOS)[None, :] == hottest_block[:, None], 8, levels)
    entry_scenario = jnp.repeat(jnp.arange(SCENARIOS, dtype=jnp.int32), CAP)
    jitter = jax.random.randint(key_jitter, (blocks, entries), 0, 4)
    scores = (jnp.take(levels, entry_scenario, axis=1) + jitter) * entries + jnp.arange(entries)[None, :]
    _, chosen = lax.top_k(scores, TOK_DEV)
    picked = jnp.take(entry_scenario, chosen, axis=0)
    order_keys = jax.random.randint(key_order, (blocks, TOK_DEV), 0, 1 << 20) * TOK_DEV + jnp.arange(TOK_DEV)[None, :]
    shuffle = jnp.argsort(order_keys, axis=1)
    picked = jnp.take_along_axis(picked, shuffle, axis=1)
    return picked.reshape(TOKENS).astype(jnp.int32)


def with_ends(result, own_key, low, top_value):
    shape = result.shape
    spot = [jax.random.randint(jax.random.fold_in(own_key, axis), (), 0, shape[axis]) for axis in range(len(shape))]
    result = result.at[tuple(spot)].set(low)
    longest = shape.index(max(shape))
    spot[longest] = (spot[longest] + 1) % shape[longest]
    return result.at[tuple(spot)].set(top_value)


def steps_of(stream_key, dims, shards, smallest, largest):
    def one(axis_at, blocks):
        heights = jax.random.uniform(jax.random.fold_in(jax.random.fold_in(stream_key, 6), axis_at), (blocks,), jnp.float32, smallest / len(shards), largest / len(shards))
        return jnp.repeat(jnp.exp(heights), dims[axis_at] // blocks).reshape((-1,) + (1,) * (len(dims) - axis_at - 1))

    factor_of = one(*shards[0])
    for cut in shards[1:]:
        factor_of = factor_of * one(*cut)
    return factor_of


def gaussian(rng, shape, spread, reach, shards=(), kind=jnp.bfloat16):
    values = jax.random.normal(rng, shape, jnp.float32) * spread
    if len(shards) > 0:
        values = steps_of(rng, shape, shards, -0.22, 0.18) * values
    return jnp.clip(values, min=-reach, max=reach).astype(kind)


def setup_inputs(seed: int = 0) -> dict:
    arg_keys = jax.random.split(jax.random.key(seed), 10)
    features = gaussian(arg_keys[0], (TOKENS, D), 1.0, 6.0, ((0, 512),))
    scenario_ids = draw_scenario_ids(jax.random.fold_in(arg_keys[9], 71), 0)
    labels = with_ends((jax.random.randint(arg_keys[2], (TASKS, TOKENS), 0, 4) < 1).astype(jnp.int32), jax.random.fold_in(arg_keys[2], 1), 0, 1)
    counts = with_ends(jax.random.randint(arg_keys[3], (SCENARIOS,), 400, 40000), jax.random.fold_in(arg_keys[3], 1), 400, 39999).astype(jnp.int32)
    scenario_weights = gaussian(arg_keys[4], (SCENARIOS, D, E), D ** -0.5, 0.5, ((0, 64),))
    shared_weights = gaussian(arg_keys[5], (D, E), D ** -0.5, 0.5)
    gate_weights = gaussian(arg_keys[6], (D, TASKS), D ** -0.5, 0.5)
    tower_weights = gaussian(arg_keys[7], (E, TASKS * TH), E ** -0.5, 0.09375)
    tower_out = gaussian(arg_keys[8], (TASKS * TH,), TH ** -0.5, 0.5)
    return dict(features=features, scenario_ids=scenario_ids, labels=labels, counts=counts, scenario_weights=scenario_weights, shared_weights=shared_weights, gate_weights=gate_weights, tower_weights=tower_weights, tower_out=tower_out)


def reference(features, scenario_ids, labels, counts, scenario_weights, shared_weights, gate_weights, tower_weights, tower_out):
    bound = TOKENS // TOK_DEV * CAP
    tower_full = tower_weights.astype(jnp.float32)
    padded_x = jnp.concatenate([features, jnp.zeros((1, D), features.dtype)], axis=0)

    def rows_of(scenario):
        row_index = jnp.nonzero(scenario_ids == scenario, size=bound, fill_value=TOKENS)[0].astype(jnp.int32)
        chosen = jnp.take(padded_x, row_index, axis=0).astype(jnp.float32)
        expert_w = lax.dynamic_index_in_dim(scenario_weights, scenario, 0, keepdims=False).astype(jnp.float32)
        hidden = jnp.maximum(jnp.dot(chosen, expert_w), 0.0).astype(jnp.bfloat16)
        return (row_index, chosen, hidden)

    def forward_step(scenario, projected):
        row_index, chosen, hidden = rows_of(scenario)
        return projected.at[row_index].set(jnp.dot(hidden.astype(jnp.float32), tower_full))
    scenario_proj = lax.fori_loop(0, SCENARIOS, forward_step, jnp.zeros((TOKENS + 1, TASKS * TH), jnp.float32))[:TOKENS]
    block_rows = TOK_DEV * 8
    blocked = features.reshape(TOKENS // block_rows, block_rows, D)

    def shared_block(inputs):
        shared_out = jnp.maximum(jnp.dot(inputs.astype(jnp.float32), shared_weights.astype(jnp.float32)), 0.0).astype(jnp.bfloat16)
        return jnp.dot(shared_out.astype(jnp.float32), tower_full)
    shared_proj = lax.map(shared_block, blocked).reshape(TOKENS, TASKS * TH)
    gate = jax.nn.sigmoid(jnp.dot(features.astype(jnp.float32), gate_weights.astype(jnp.float32)))
    gate_cols = jnp.repeat(gate, TH, axis=1)
    tower_in = gate_cols * scenario_proj + (1.0 - gate_cols) * shared_proj
    tower_act = jnp.maximum(tower_in, 0.0).astype(jnp.bfloat16)
    out_full = tower_out.astype(jnp.float32)
    terms = tower_act.astype(jnp.float32) * out_full[None, :]
    logit_rows = lax.optimization_barrier(jnp.sum(terms.reshape(TOKENS, TASKS, TH), axis=2))
    weight_table = 64.0 / jnp.sqrt(counts.astype(jnp.float32))
    weight = jnp.take(weight_table, scenario_ids, axis=0)
    dlogit = weight[:, None] * (jax.nn.sigmoid(logit_rows) - labels.T.astype(jnp.float32))
    mixed_grad = jnp.where(tower_in > 0.0, gate_cols * jnp.repeat(dlogit, TH, axis=1) * out_full[None, :], 0.0).astype(jnp.bfloat16)
    padded_grad = jnp.concatenate([mixed_grad, jnp.zeros((1, TASKS * TH), jnp.bfloat16)], axis=0)

    def backward_step(scenario):
        row_index, chosen, hidden = rows_of(scenario)
        grad_rows = jnp.take(padded_grad, row_index, axis=0).astype(jnp.float32)
        expert_grad = jnp.dot(grad_rows, tower_full.T).astype(jnp.bfloat16)
        masked = jnp.where(hidden > 0.0, expert_grad, jnp.zeros_like(expert_grad)).astype(jnp.float32)
        return jnp.dot(chosen.T, masked)
    scenario_grad = lax.map(backward_step, jnp.arange(SCENARIOS, dtype=jnp.int32))
    return (logit_rows.T, scenario_grad)
```

```python
import functools

import jax
import jax.numpy as jnp
from jax import lax
from jax.experimental import pallas as pl
from jax.experimental.pallas import tpu as pltpu
from jax.sharding import PartitionSpec as P

MESH = pl.DeviceIdType.MESH
CAP = 8
LANES = 128
CHUNKS = 4


def dot(a, b, dims=((1,), (0,)), precision=None):
    return lax.dot_general(a, b, (dims, ((), ())), precision=precision, preferred_element_type=jnp.float32)


def iota(shape, dim):
    return lax.broadcasted_iota(jnp.int32, shape, dim)


def step_kernel(
    owners,
    groups,
    ids_ref,
    labels_ref,
    feats_ref,
    counts_ref,
    w_hbm,
    s_hbm,
    gate_ref,
    t_hbm,
    tout_ref,
    logits_ref,
    grad_ref,
    w_ref,
    s_ref,
    t_ref,
    out_x,
    x_ref,
    lab_s,
    lab_r,
    lg_s,
    lg_r,
    hidden,
    proj,
    core_s,
    core_r,
    core_f,
    link_s,
    link_r,
    load_sem,
    x_send,
    x_recv,
    lab_send,
    lab_recv,
    lg_send,
    lg_recv,
    core_send,
    core_recv,
    link_send,
    link_recv,
):
    own = lax.axis_index("own")
    grp = lax.axis_index("grp")
    core = lax.rem(grp, 2)
    chip = lax.div(grp, 2)
    chips = groups // 2
    partner = (grp + 1 - 2 * core, own)
    half = owners // 2
    quarter = owners // 4
    tokens, width = feats_ref.shape
    expert = w_ref.shape[1]
    cols = expert // CHUNKS
    rows = owners * CAP
    part = width // groups

    barrier = pltpu.get_barrier_semaphore()

    def greet(i, carry):
        pl.semaphore_signal(barrier, inc=1, device_id=(grp, lax.rem(own + i, owners)), device_id_type=MESH)
        return carry

    lax.fori_loop(1, owners, greet, 0)
    pl.semaphore_signal(barrier, inc=1, device_id=partner, device_id_type=MESH)
    for d in range(1, chips):
        pl.semaphore_signal(barrier, inc=1, device_id=(lax.rem(grp + 2 * d, groups), own), device_id_type=MESH)

    loads = [
        pltpu.make_async_copy(w_hbm.at[0], w_ref, load_sem.at[0]),
        pltpu.make_async_copy(s_hbm, s_ref, load_sem.at[1]),
        pltpu.make_async_copy(t_hbm, t_ref, load_sem.at[2]),
    ]
    for load in loads:
        load.start()

    ids = ids_ref[...]
    member = iota((owners, tokens), 0) == ids
    member_b = member.astype(jnp.float32).astype(jnp.bfloat16)
    before = (iota((tokens, tokens), 0) < iota((tokens, tokens), 1)).astype(jnp.float32).astype(jnp.bfloat16)
    earlier = dot(member_b, before)
    rank = jnp.sum(jnp.where(member, earlier, 0.0), axis=0, keepdims=True).astype(jnp.int32)
    slot = ids * CAP + rank
    place = (iota((rows, tokens), 0) == slot).astype(jnp.float32).astype(jnp.bfloat16)
    out_x[...] = dot(place, feats_ref[...]).astype(jnp.bfloat16).reshape(owners, CAP, width)
    lane_t = iota((LANES, tokens), 0)
    labels_f = labels_ref[...].astype(jnp.float32)
    label_of = jnp.where(lax.rem(lane_t, 2) == 0, labels_f[0:1], labels_f[1:2])
    label_at = jnp.where(lax.div(lane_t, 2) == rank, label_of, 0.0).astype(jnp.bfloat16)
    lab_s[...] = dot(member_b, label_at, ((1,), (1,))).reshape(owners, 1, LANES)

    pl.semaphore_wait(barrier, owners - 1 + 1 + chips - 1)

    def offset_of(i):
        k = lax.div(i + 1, 2)
        return half - k + 2 * k * lax.rem(i, 2)

    def send_x(group):
        def body(i, carry):
            off = offset_of(i)
            target = lax.rem(own + off, owners)
            spot = lax.rem(owners + quarter - off, owners)
            pltpu.make_async_remote_copy(
                out_x.at[target], x_ref.at[spot], x_send, x_recv.at[group], device_id=(grp, target), device_id_type=MESH
            ).start()
            return carry

        return body

    lax.fori_loop(0, half, send_x(0), 0)
    lax.fori_loop(half, owners - 1, send_x(1), 0)

    def send_label(i, carry):
        off = offset_of(i)
        target = lax.rem(own + off, owners)
        spot = lax.rem(owners + quarter - off, owners)
        pltpu.make_async_remote_copy(
            lab_s.at[target], lab_r.at[spot], lab_send, lab_recv, device_id=(grp, target), device_id_type=MESH
        ).start()
        return carry

    lax.fori_loop(0, owners - 1, send_label, 0)
    x_ref[quarter] = out_x[own]
    lab_r[quarter] = lab_s[own]

    def bulk(src, dst, count, send, recv):
        return pltpu.make_async_remote_copy(
            src.at[pl.ds(0, count)], dst.at[pl.ds(0, count)], send, recv, device_id=partner, device_id_type=MESH
        )

    for load in loads:
        load.wait()

    task_of = lax.div(iota((1, 2 * LANES), 1), LANES)
    gate_b = jnp.where(
        task_of == 0,
        jnp.broadcast_to(gate_ref[:, 0:1].astype(jnp.float32), (width, 2 * LANES)),
        jnp.broadcast_to(gate_ref[:, 1:2].astype(jnp.float32), (width, 2 * LANES)),
    ).astype(jnp.bfloat16)
    tout = tout_ref[...].astype(jnp.float32)
    same_task = lax.div(iota((2 * LANES, 2 * LANES), 0), LANES) == lax.div(iota((2 * LANES, 2 * LANES), 1), LANES)
    tout_b = jnp.where(same_task, tout, 0.0).astype(jnp.bfloat16)

    def forward(group):
        x = x_ref[pl.ds(group * half, half)].reshape(half * CAP, width)
        block = half * CAP
        acc = None
        for c in range(CHUNKS):
            at = pl.ds(c * cols, cols)
            h = jnp.maximum(dot(x, w_ref[:, at]), 0.0).astype(jnp.bfloat16)
            s = jnp.maximum(dot(x, s_ref[:, at]), 0.0).astype(jnp.bfloat16)
            hidden[pl.ds(group * block, block), at] = h
            more = dot(jnp.concatenate([h, s], axis=0), t_ref[at, :])
            acc = more if acc is None else acc + more
        gate = jax.nn.sigmoid(dot(x, gate_b))
        return acc[:block], acc[block:], gate

    bulk(out_x, x_ref, half - 1, x_send, x_recv.at[1]).wait_recv()
    p_near = forward(0)
    bulk(out_x, x_ref, half, x_send, x_recv.at[0]).wait_recv()
    p_far = forward(1)
    scen, shared, gate = (jnp.concatenate([a, b], axis=0) for a, b in zip(p_near, p_far))
    tower_in = gate * scen + (1.0 - gate) * shared
    act = jnp.maximum(tower_in, 0.0).astype(jnp.bfloat16)
    logit = dot(act, tout_b, ((1,), (1,)))

    lane = iota((rows, LANES), 1)
    mine = lax.rem(iota((rows, LANES), 0), CAP) == lax.div(lane, 2)
    pick = jnp.where(lax.rem(lane, 2) == 0, logit[:, :LANES], logit[:, LANES:])
    lg_s[...] = jnp.sum(jnp.where(mine, pick, 0.0).reshape(owners, CAP, LANES), axis=1, keepdims=True)

    def send_logit(i, carry):
        off = offset_of(i)
        target = lax.rem(own + off, owners)
        spot = lax.rem(off + quarter, owners)
        pltpu.make_async_remote_copy(
            lg_s.at[spot], lg_r.at[own], lg_send, lg_recv, device_id=(grp, target), device_id_type=MESH
        ).start()
        return carry

    lax.fori_loop(0, owners - 1, send_logit, 0)
    lg_r[own] = lg_s[quarter]

    bulk(lab_s, lab_r, owners - 1, lab_send, lab_recv).wait_recv()
    spread = (lax.div(iota((rows, owners), 0), CAP) == iota((rows, owners), 1)).astype(jnp.float32).astype(jnp.bfloat16)
    packed = dot(spread, lab_r[...].reshape(owners, LANES).astype(jnp.bfloat16))
    packed = jnp.where(mine, packed, 0.0).astype(jnp.bfloat16)
    fan = (lax.rem(iota((LANES, 2 * LANES), 0), 2) == lax.div(iota((LANES, 2 * LANES), 1), LANES)).astype(jnp.float32).astype(jnp.bfloat16)
    label = dot(packed, fan)
    weight = 64.0 / jnp.sqrt(jnp.full((1, 2 * LANES), counts_ref[own], jnp.int32).astype(jnp.float32))
    dlogit = weight * (jax.nn.sigmoid(logit) - label)
    mixed = jnp.where(tower_in > 0.0, gate * dlogit * tout, 0.0).astype(jnp.bfloat16)

    d_new = iota((width, width), 0)
    d_old = iota((width, width), 1)
    from_row = (2 * lax.rem(lax.div(d_new, part), chips) + lax.div(d_new, part * chips)) * part + lax.rem(d_new, part)
    order = (d_old == from_row).astype(jnp.float32).astype(jnp.bfloat16)
    x_t = dot(order, x_ref[...].reshape(rows, width), ((1,), (1,))).astype(jnp.bfloat16)

    def core_copy(c):
        return pltpu.make_async_remote_copy(
            core_s.at[c, 1 - core], core_r.at[c], core_send.at[c], core_recv.at[c], device_id=partner, device_id_type=MESH
        )

    def link_copy(c, d):
        to = lax.rem(chip + d, chips)
        return pltpu.make_async_remote_copy(
            link_s.at[c, to],
            link_r.at[c, d - 1],
            link_send.at[c, d - 1],
            link_recv.at[c, d - 1],
            device_id=(2 * to + core, own),
            device_id_type=MESH,
        )

    def relay(c):
        core_copy(c).wait_recv()
        total = core_f[c, core] + core_r[c].astype(jnp.float32)
        proj[c] = total.reshape(chips, part, cols)
        link_s[c] = total.astype(jnp.bfloat16).reshape(chips, part, cols)
        for d in (2, 1, 3):
            link_copy(c, d).start()

    for c in range(CHUNKS):
        at = pl.ds(c * cols, cols)
        back = dot(mixed, t_ref[at, :], ((1,), (1,))).astype(jnp.bfloat16)
        masked = jnp.where(hidden[:, at] > 0.0, back, jnp.zeros_like(back))
        share = dot(x_t, masked)
        core_f[c] = share.reshape(2, width // 2, cols)
        core_s[c] = share.astype(jnp.bfloat16).reshape(2, width // 2, cols)
        core_copy(c).start()
        if c > 0:
            relay(c - 1)
    relay(CHUNKS - 1)
    for c in range(CHUNKS):
        total = proj[c, chip]
        for d in range(1, chips):
            link_copy(c, d).wait_recv()
            total = total + link_r[c, d - 1].astype(jnp.float32)
        grad_ref[0, :, pl.ds(c * cols, cols)] = total

    bulk(lg_s, lg_r, owners - 1, lg_send, lg_recv).wait_recv()
    got = lg_r[...].reshape(owners, LANES)
    found = dot(got, member.astype(jnp.float32), ((0,), (0,)), lax.Precision.HIGHEST)
    for task in range(2):
        logits_ref[pl.ds(task, 1), :] = jnp.sum(jnp.where(lane_t == 2 * rank + task, found, 0.0), axis=0, keepdims=True)

    bulk(out_x, x_ref, owners - 1, x_send, x_recv.at[0]).wait_send()
    bulk(lab_s, lab_r, owners - 1, lab_send, lab_recv).wait_send()
    bulk(lg_s, lg_r, owners - 1, lg_send, lg_recv).wait_send()
    for c in range(CHUNKS):
        core_copy(c).wait_send()
        for d in range(1, chips):
            link_copy(c, d).wait_send()


def shards(owners, groups, features, scenario_ids, labels, counts, scenario_weights, shared_weights, gate_weights, tower_weights, tower_out):
    tokens, width = features.shape
    expert, towers = tower_weights.shape
    cols = expert // CHUNKS
    part = width // groups
    chips = groups // 2
    vmem = pl.BlockSpec(memory_space=pltpu.VMEM)
    hbm = pl.BlockSpec(memory_space=pl.ANY)
    dma = pltpu.SemaphoreType.DMA
    bf16, f32 = jnp.bfloat16, jnp.float32
    return pl.pallas_call(
        functools.partial(step_kernel, owners, groups),
        out_shape=(
            jax.ShapeDtypeStruct((2, tokens), f32),
            jax.ShapeDtypeStruct((1, part, expert), f32),
        ),
        in_specs=[vmem, vmem, vmem, pl.BlockSpec(memory_space=pltpu.SMEM), hbm, hbm, vmem, hbm, vmem],
        out_specs=(vmem, vmem),
        scratch_shapes=[
            pltpu.VMEM((width, expert), bf16),
            pltpu.VMEM((width, expert), bf16),
            pltpu.VMEM((expert, towers), bf16),
            pltpu.VMEM((owners, CAP, width), bf16),
            pltpu.VMEM((owners, CAP, width), bf16),
            pltpu.VMEM((owners, 1, LANES), f32),
            pltpu.VMEM((owners, 1, LANES), f32),
            pltpu.VMEM((owners, 1, LANES), f32),
            pltpu.VMEM((owners, 1, LANES), f32),
            pltpu.VMEM((owners * CAP, expert), bf16),
            pltpu.VMEM((CHUNKS, chips, part, cols), f32),
            pltpu.VMEM((CHUNKS, 2, width // 2, cols), bf16),
            pltpu.VMEM((CHUNKS, width // 2, cols), bf16),
            pltpu.VMEM((CHUNKS, 2, width // 2, cols), f32),
            pltpu.VMEM((CHUNKS, chips, part, cols), bf16),
            pltpu.VMEM((CHUNKS, chips - 1, part, cols), bf16),
            dma((3,)),
            dma(()),
            dma((2,)),
            dma(()),
            dma(()),
            dma(()),
            dma(()),
            dma((CHUNKS,)),
            dma((CHUNKS,)),
            dma((CHUNKS, chips - 1)),
            dma((CHUNKS, chips - 1)),
        ],
        compiler_params=pltpu.CompilerParams(collective_id=0, has_side_effects=True, vmem_limit_bytes=56 * 1024 * 1024),
    )(
        scenario_ids.reshape(1, tokens),
        labels,
        features,
        counts,
        scenario_weights,
        shared_weights,
        gate_weights,
        tower_weights,
        tower_out.reshape(1, towers),
    )


def solution(mesh):
    return jax.shard_map(
        functools.partial(shards, mesh.shape["own"], mesh.shape["grp"]),
        mesh=mesh,
        in_specs=(
            P(("grp", "own"), None),
            P(("grp", "own")),
            P(None, ("grp", "own")),
            P(),
            P("own", None, None),
            P(),
            P(),
            P(),
            P(),
        ),
        out_specs=(P(None, ("grp", "own")), P("own", "grp", None)),
        check_vma=False,
    )
```

```python
import functools

import jax
import jax.numpy as jnp
from jax import lax
from jax.experimental import pallas as pl
from jax.experimental.pallas import tpu as pltpu
from jax.sharding import PartitionSpec as P

MESH = pl.DeviceIdType.MESH
CAP = 8
YS = 4
REACH = 4
LANES = 128
CHUNKS = 4


def dot(a, b, dims=((1,), (0,)), precision=None):
    return lax.dot_general(a, b, (dims, ((), ())), precision=precision, preferred_element_type=jnp.float32)


def iota(shape, dim):
    return lax.broadcasted_iota(jnp.int32, shape, dim)


def step_kernel(
    owners,
    groups,
    ids_ref,
    labels_ref,
    feats_ref,
    counts_ref,
    w_hbm,
    s_hbm,
    gate_ref,
    t_hbm,
    tout_ref,
    logits_ref,
    grad_ref,
    w_ref,
    s_ref,
    t_ref,
    out_x,
    x_ref,
    lab_s,
    lab_r,
    lg_s,
    lg_r,
    hidden,
    proj,
    core_s,
    core_r,
    core_f,
    link_s,
    link_r,
    load_sem,
    x_send,
    x_recv,
    lab_send,
    lab_recv,
    lg_send,
    lg_recv,
    near_sem,
    core_send,
    core_recv,
    link_send,
    link_recv,
):
    own = lax.axis_index("own")
    grp = lax.axis_index("grp")
    core = lax.rem(grp, 2)
    chip = lax.div(grp, 2)
    chips = groups // 2
    partner = (grp + 1 - 2 * core, own)
    zs = owners // YS
    z = lax.div(own, YS)
    y = lax.rem(own, YS)
    turn = REACH * YS
    near = 2 * turn + YS
    far = owners - near
    tokens, width = feats_ref.shape
    expert = w_ref.shape[1]
    cols = expert // CHUNKS
    rows = owners * CAP
    part = width // groups

    barrier = pltpu.get_barrier_semaphore()

    def near_offset(i):
        k = lax.div(i, 2)
        off = jnp.where(lax.rem(i, 2) == 0, turn + YS - 1 - k, owners - turn + k)
        return jnp.where(off == owners, 1, off)

    def far_offset(i):
        k = lax.div(i, 2)
        return jnp.where(lax.rem(i, 2) == 0, turn + YS + far // 2 - 1 - k, turn + YS + far // 2 + k)

    def spot_of(off):
        return lax.rem(off + turn, owners)

    def ahead(off):
        return lax.rem(z + lax.div(off, YS), zs) * YS + lax.rem(y + lax.rem(off, YS), YS)

    def behind(off):
        return lax.rem(z + zs - lax.div(off, YS), zs) * YS + lax.rem(y + YS - lax.rem(off, YS), YS)

    def greet(i, carry):
        pl.semaphore_signal(barrier, inc=1, device_id=(grp, ahead(near_offset(i))), device_id_type=MESH)
        return carry

    lax.fori_loop(0, near - 1, greet, 0)
    pl.semaphore_signal(barrier, inc=1, device_id=partner, device_id_type=MESH)
    for d in range(1, chips):
        pl.semaphore_signal(barrier, inc=1, device_id=(lax.rem(grp + 2 * d, groups), own), device_id_type=MESH)

    loads = [
        pltpu.make_async_copy(w_hbm.at[0], w_ref, load_sem.at[0]),
        pltpu.make_async_copy(s_hbm, s_ref, load_sem.at[1]),
        pltpu.make_async_copy(t_hbm, t_ref, load_sem.at[2]),
    ]
    for load in loads:
        load.start()

    ids = ids_ref[...]
    to_z = lax.rem(lax.div(ids, YS) - z + zs, zs)
    to_y = lax.rem(lax.rem(ids, YS) - y + YS, YS)
    spots = spot_of(to_z * YS + to_y)
    member = iota((owners, tokens), 0) == spots
    member_b = member.astype(jnp.float32).astype(jnp.bfloat16)
    before = (iota((tokens, tokens), 0) < iota((tokens, tokens), 1)).astype(jnp.float32).astype(jnp.bfloat16)
    earlier = dot(member_b, before)
    rank = jnp.sum(jnp.where(member, earlier, 0.0), axis=0, keepdims=True).astype(jnp.int32)
    slot = spots * CAP + rank
    place = (iota((rows, tokens), 0) == slot).astype(jnp.float32).astype(jnp.bfloat16)
    out_x[...] = dot(place, feats_ref[...]).astype(jnp.bfloat16).reshape(owners, CAP, width)
    lane_t = iota((LANES, tokens), 0)
    labels_f = labels_ref[...].astype(jnp.float32)
    label_of = jnp.where(lax.rem(lane_t, 2) == 0, labels_f[0:1], labels_f[1:2])
    label_at = jnp.where(lax.div(lane_t, 2) == rank, label_of, 0.0).astype(jnp.bfloat16)
    lab_s[...] = dot(member_b, label_at, ((1,), (1,))).reshape(owners, 1, LANES)

    def send_x(offset, group):
        def body(i, carry):
            off = offset(i)
            spot = spot_of(off)
            pltpu.make_async_remote_copy(
                out_x.at[spot], x_ref.at[spot], x_send, x_recv.at[group], device_id=(grp, ahead(off)), device_id_type=MESH
            ).start()
            return carry

        return body

    def send_label(offset):
        def body(i, carry):
            off = offset(i)
            spot = spot_of(off)
            pltpu.make_async_remote_copy(
                lab_s.at[spot], lab_r.at[spot], lab_send, lab_recv, device_id=(grp, ahead(off)), device_id_type=MESH
            ).start()
            return carry

        return body

    pl.semaphore_wait(barrier, near - 1 + 1 + chips - 1)
    for end in (REACH, zs - REACH):
        pl.semaphore_signal(near_sem, inc=1, device_id=(grp, lax.rem(z + end, zs) * YS + y), device_id_type=MESH)
    lax.fori_loop(0, near - 1, send_x(near_offset, 0), 0)
    pl.semaphore_wait(near_sem, 2)
    lax.fori_loop(0, far, send_x(far_offset, 1), 0)
    lax.fori_loop(0, near - 1, send_label(near_offset), 0)
    lax.fori_loop(0, far, send_label(far_offset), 0)
    x_ref[turn] = out_x[turn]
    lab_r[turn] = lab_s[turn]

    def bulk(src, dst, count, send, recv):
        return pltpu.make_async_remote_copy(
            src.at[pl.ds(0, count)], dst.at[pl.ds(0, count)], send, recv, device_id=partner, device_id_type=MESH
        )

    for load in loads:
        load.wait()

    task_row = lax.div(iota((2 * LANES, 1), 0), LANES)
    gate_w = gate_ref[...].astype(jnp.float32)
    gate_b = jnp.where(task_row == 0, gate_w[0:1], gate_w[1:2]).astype(jnp.bfloat16)
    tout_w = tout_ref[...].astype(jnp.float32)
    tout = jnp.concatenate([tout_w[0:1], tout_w[1:2]], axis=1)
    same_task = lax.div(iota((2 * LANES, 2 * LANES), 0), LANES) == lax.div(iota((2 * LANES, 2 * LANES), 1), LANES)
    tout_b = jnp.where(same_task, tout, 0.0).astype(jnp.bfloat16)

    def own_lane(blocks):
        lane = iota((blocks * CAP, LANES), 1)
        return lane, lax.rem(iota((blocks * CAP, LANES), 0), CAP) == lax.div(lane, 2)

    def forward(first, blocks):
        x = x_ref[pl.ds(first, blocks)].reshape(blocks * CAP, width)
        block = blocks * CAP
        acc = None
        for c in range(CHUNKS):
            at = pl.ds(c * cols, cols)
            h = jnp.maximum(dot(x, w_ref[:, at]), 0.0).astype(jnp.bfloat16)
            s = jnp.maximum(dot(x, s_ref[:, at]), 0.0).astype(jnp.bfloat16)
            hidden[pl.ds(first * CAP, block), at] = h
            more = dot(jnp.concatenate([h, s], axis=0), t_ref[at, :])
            acc = more if acc is None else acc + more
        gate = jax.nn.sigmoid(dot(x, gate_b, ((1,), (1,))))
        tower_in = gate * acc[:block] + (1.0 - gate) * acc[block:]
        act = jnp.maximum(tower_in, 0.0).astype(jnp.bfloat16)
        logit = dot(act, tout_b, ((1,), (1,)))
        lane, mine = own_lane(blocks)
        pick = jnp.where(lax.rem(lane, 2) == 0, logit[:, :LANES], logit[:, LANES:])
        lg_s[pl.ds(first, blocks)] = jnp.sum(
            jnp.where(mine, pick, 0.0).reshape(blocks, CAP, LANES), axis=1, keepdims=True
        )
        return gate, tower_in, logit

    def send_logit(offset):
        def body(i, carry):
            off = offset(i)
            spot = spot_of(off)
            pltpu.make_async_remote_copy(
                lg_s.at[spot], lg_r.at[spot], lg_send, lg_recv, device_id=(grp, behind(off)), device_id_type=MESH
            ).start()
            return carry

        return body

    bulk(out_x, x_ref, near - 1, x_send, x_recv.at[0]).wait_recv()
    near_side = forward(0, near)
    lax.fori_loop(0, near - 1, send_logit(near_offset), 0)
    lg_r[turn] = lg_s[turn]
    bulk(out_x, x_ref, far, x_send, x_recv.at[1]).wait_recv()
    far_side = forward(near, far)
    lax.fori_loop(0, far, send_logit(far_offset), 0)

    bulk(lab_s, lab_r, owners - 1, lab_send, lab_recv).wait_recv()
    spread = (lax.div(iota((rows, owners), 0), CAP) == iota((rows, owners), 1)).astype(jnp.float32).astype(jnp.bfloat16)
    packed = dot(spread, lab_r[...].reshape(owners, LANES).astype(jnp.bfloat16))
    packed = jnp.where(own_lane(owners)[1], packed, 0.0).astype(jnp.bfloat16)
    fan = (lax.rem(iota((LANES, 2 * LANES), 0), 2) == lax.div(iota((LANES, 2 * LANES), 1), LANES)).astype(jnp.float32).astype(jnp.bfloat16)
    label = dot(packed, fan)
    weight = 64.0 / jnp.sqrt(jnp.full((1, 2 * LANES), counts_ref[own], jnp.int32).astype(jnp.float32))

    def gradient(side, label):
        gate, tower_in, logit = side
        dlogit = weight * (jax.nn.sigmoid(logit) - label)
        return jnp.where(tower_in > 0.0, gate * dlogit * tout, 0.0).astype(jnp.bfloat16)

    mixed = jnp.concatenate(
        [gradient(near_side, label[: near * CAP]), gradient(far_side, label[near * CAP :])], axis=0
    )

    d_new = iota((width, width), 0)
    d_old = iota((width, width), 1)
    from_row = (2 * lax.rem(lax.div(d_new, part), chips) + lax.div(d_new, part * chips)) * part + lax.rem(d_new, part)
    order = (d_old == from_row).astype(jnp.float32).astype(jnp.bfloat16)
    x_t = dot(order, x_ref[...].reshape(rows, width), ((1,), (1,))).astype(jnp.bfloat16)

    def core_copy(c):
        return pltpu.make_async_remote_copy(
            core_s.at[c, 1 - core], core_r.at[c], core_send.at[c], core_recv.at[c], device_id=partner, device_id_type=MESH
        )

    def link_copy(c, d):
        to = lax.rem(chip + d, chips)
        return pltpu.make_async_remote_copy(
            link_s.at[c, to],
            link_r.at[c, d - 1],
            link_send.at[c, d - 1],
            link_recv.at[c, d - 1],
            device_id=(2 * to + core, own),
            device_id_type=MESH,
        )

    def relay(c):
        core_copy(c).wait_recv()
        total = core_f[c, core] + core_r[c].astype(jnp.float32)
        proj[c] = total.reshape(chips, part, cols)
        link_s[c] = total.astype(jnp.bfloat16).reshape(chips, part, cols)
        for d in (2, 1, 3):
            link_copy(c, d).start()

    for c in range(CHUNKS):
        at = pl.ds(c * cols, cols)
        back = dot(mixed, t_ref[at, :], ((1,), (1,))).astype(jnp.bfloat16)
        masked = jnp.where(hidden[:, at] > 0.0, back, jnp.zeros_like(back))
        share = dot(x_t, masked)
        core_f[c] = share.reshape(2, width // 2, cols)
        core_s[c] = share.astype(jnp.bfloat16).reshape(2, width // 2, cols)
        core_copy(c).start()
        if c > 0:
            relay(c - 1)
    relay(CHUNKS - 1)
    for c in range(CHUNKS):
        total = proj[c, chip]
        for d in range(1, chips):
            link_copy(c, d).wait_recv()
            total = total + link_r[c, d - 1].astype(jnp.float32)
        grad_ref[0, :, pl.ds(c * cols, cols)] = total

    bulk(lg_s, lg_r, owners - 1, lg_send, lg_recv).wait_recv()
    got = lg_r[...].reshape(owners, LANES)
    found = dot(got, member.astype(jnp.float32), ((0,), (0,)), lax.Precision.HIGHEST)
    for task in range(2):
        logits_ref[pl.ds(task, 1), :] = jnp.sum(jnp.where(lane_t == 2 * rank + task, found, 0.0), axis=0, keepdims=True)

    bulk(out_x, x_ref, owners - 1, x_send, x_recv.at[0]).wait_send()
    bulk(lab_s, lab_r, owners - 1, lab_send, lab_recv).wait_send()
    bulk(lg_s, lg_r, owners - 1, lg_send, lg_recv).wait_send()
    for c in range(CHUNKS):
        core_copy(c).wait_send()
        for d in range(1, chips):
            link_copy(c, d).wait_send()


def shards(owners, groups, features, scenario_ids, labels, counts, scenario_weights, shared_weights, gate_weights, tower_weights, tower_out):
    tokens, width = features.shape
    expert, towers = tower_weights.shape
    cols = expert // CHUNKS
    part = width // groups
    chips = groups // 2
    vmem = pl.BlockSpec(memory_space=pltpu.VMEM)
    hbm = pl.BlockSpec(memory_space=pl.ANY)
    dma = pltpu.SemaphoreType.DMA
    bf16, f32 = jnp.bfloat16, jnp.float32
    return pl.pallas_call(
        functools.partial(step_kernel, owners, groups),
        out_shape=(pltpu.VMEM((2, tokens), f32), pltpu.VMEM((1, part, expert), f32)),
        in_specs=[vmem, vmem, vmem, pl.BlockSpec(memory_space=pltpu.SMEM), hbm, hbm, vmem, hbm, vmem],
        out_specs=(vmem, vmem),
        scratch_shapes=[
            pltpu.VMEM((width, expert), bf16),
            pltpu.VMEM((width, expert), bf16),
            pltpu.VMEM((expert, towers), bf16),
            pltpu.VMEM((owners, CAP, width), bf16),
            pltpu.VMEM((owners, CAP, width), bf16),
            pltpu.VMEM((owners, 1, LANES), f32),
            pltpu.VMEM((owners, 1, LANES), f32),
            pltpu.VMEM((owners, 1, LANES), f32),
            pltpu.VMEM((owners, 1, LANES), f32),
            pltpu.VMEM((owners * CAP, expert), bf16),
            pltpu.VMEM((CHUNKS, chips, part, cols), f32),
            pltpu.VMEM((CHUNKS, 2, width // 2, cols), bf16),
            pltpu.VMEM((CHUNKS, width // 2, cols), bf16),
            pltpu.VMEM((CHUNKS, 2, width // 2, cols), f32),
            pltpu.VMEM((CHUNKS, chips, part, cols), bf16),
            pltpu.VMEM((CHUNKS, chips - 1, part, cols), bf16),
            dma((3,)),
            dma(()),
            dma((2,)),
            dma(()),
            dma(()),
            dma(()),
            dma(()),
            pltpu.SemaphoreType.REGULAR,
            dma((CHUNKS,)),
            dma((CHUNKS,)),
            dma((CHUNKS, chips - 1)),
            dma((CHUNKS, chips - 1)),
        ],
        compiler_params=pltpu.CompilerParams(collective_id=0, has_side_effects=True, vmem_limit_bytes=56 * 1024 * 1024),
    )(
        scenario_ids.reshape(1, tokens),
        labels,
        features,
        counts,
        scenario_weights,
        shared_weights,
        gate_weights.T,
        tower_weights,
        tower_out.reshape(2, towers // 2),
    )


def solution(mesh):
    return jax.shard_map(
        functools.partial(shards, mesh.shape["own"], mesh.shape["grp"]),
        mesh=mesh,
        in_specs=(
            P(("grp", "own"), None),
            P(("grp", "own")),
            P(None, ("grp", "own")),
            P(),
            P("own", None, None),
            P(),
            P(),
            P(),
            P(),
        ),
        out_specs=(P(None, ("grp", "own")), P("own", "grp", None)),
        check_vma=False,
    )
```

```python
import functools

import jax
import jax.numpy as jnp
from jax import lax
from jax.experimental import pallas as pl
from jax.experimental.pallas import tpu as pltpu
from jax.sharding import PartitionSpec as P

MESH = pl.DeviceIdType.MESH
CAP = 8
YS = 4
REACH = 4
LANES = 128
CHUNKS = 4


def dot(a, b, dims=((1,), (0,)), precision=None):
    return lax.dot_general(a, b, (dims, ((), ())), precision=precision, preferred_element_type=jnp.float32)


def iota(shape, dim):
    return lax.broadcasted_iota(jnp.int32, shape, dim)


def step_kernel(
    owners,
    groups,
    ids_ref,
    labels_ref,
    feats_ref,
    counts_ref,
    w_hbm,
    s_hbm,
    gate_ref,
    t_hbm,
    tout_ref,
    logits_ref,
    grad_ref,
    w_ref,
    s_ref,
    t_ref,
    out_x,
    x_ref,
    lab_s,
    lab_r,
    lg_s,
    lg_r,
    hidden,
    proj,
    core_s,
    core_r,
    core_f,
    link_s,
    link_r,
    sum_s,
    sum_r,
    load_sem,
    x_send,
    x_recv,
    lab_send,
    lab_recv,
    lg_send,
    lg_recv,
    near_sem,
    core_send,
    core_recv,
    link_send,
    link_recv,
    sum_send,
    sum_recv,
):
    own = lax.axis_index("own")
    grp = lax.axis_index("grp")
    core = lax.rem(grp, 2)
    chip = lax.div(grp, 2)
    chips = groups // 2
    partner = (grp + 1 - 2 * core, own)
    zs = owners // YS
    z = lax.div(own, YS)
    y = lax.rem(own, YS)
    turn = REACH * YS
    near = 2 * turn + YS
    far = owners - near
    tokens, width = feats_ref.shape
    expert = w_ref.shape[1]
    cols = expert // CHUNKS
    rows = owners * CAP
    part = width // groups

    barrier = pltpu.get_barrier_semaphore()

    def near_offset(i):
        k = lax.div(i, 2)
        off = jnp.where(lax.rem(i, 2) == 0, turn + YS - 1 - k, owners - turn + k)
        return jnp.where(off == owners, 1, off)

    def far_offset(i):
        k = lax.div(i, 2)
        return jnp.where(lax.rem(i, 2) == 0, turn + YS + far // 2 - 1 - k, turn + YS + far // 2 + k)

    def spot_of(off):
        return lax.rem(off + turn, owners)

    def ahead(off):
        return lax.rem(z + lax.div(off, YS), zs) * YS + lax.rem(y + lax.rem(off, YS), YS)

    def behind(off):
        return lax.rem(z + zs - lax.div(off, YS), zs) * YS + lax.rem(y + YS - lax.rem(off, YS), YS)

    def greet(i, carry):
        pl.semaphore_signal(barrier, inc=1, device_id=(grp, ahead(near_offset(i))), device_id_type=MESH)
        return carry

    lax.fori_loop(0, near - 1, greet, 0)
    pl.semaphore_signal(barrier, inc=1, device_id=partner, device_id_type=MESH)
    for d in range(1, chips):
        pl.semaphore_signal(barrier, inc=1, device_id=(lax.rem(grp + 2 * d, groups), own), device_id_type=MESH)

    loads = [
        pltpu.make_async_copy(w_hbm.at[0], w_ref, load_sem.at[0]),
        pltpu.make_async_copy(s_hbm, s_ref, load_sem.at[1]),
        pltpu.make_async_copy(t_hbm, t_ref, load_sem.at[2]),
    ]
    for load in loads:
        load.start()

    ids = ids_ref[...]
    to_z = lax.rem(lax.div(ids, YS) - z + zs, zs)
    to_y = lax.rem(lax.rem(ids, YS) - y + YS, YS)
    spots = spot_of(to_z * YS + to_y)
    member = iota((owners, tokens), 0) == spots
    member_b = member.astype(jnp.float32).astype(jnp.bfloat16)
    before = (iota((tokens, tokens), 0) < iota((tokens, tokens), 1)).astype(jnp.float32).astype(jnp.bfloat16)
    earlier = dot(member_b, before)
    rank = jnp.sum(jnp.where(member, earlier, 0.0), axis=0, keepdims=True).astype(jnp.int32)
    slot = spots * CAP + rank
    place = (iota((rows, tokens), 0) == slot).astype(jnp.float32).astype(jnp.bfloat16)
    out_x[...] = dot(place, feats_ref[...]).astype(jnp.bfloat16).reshape(owners, CAP, width)
    lane_t = iota((LANES, tokens), 0)
    labels_f = labels_ref[...].astype(jnp.float32)
    label_of = jnp.where(lax.rem(lane_t, 2) == 0, labels_f[0:1], labels_f[1:2])
    label_at = jnp.where(lax.div(lane_t, 2) == rank, label_of, 0.0).astype(jnp.bfloat16)
    lab_s[...] = dot(member_b, label_at, ((1,), (1,))).reshape(owners, 1, LANES)

    def send_x(offset, group):
        def body(i, carry):
            off = offset(i)
            spot = spot_of(off)
            pltpu.make_async_remote_copy(
                out_x.at[spot], x_ref.at[spot], x_send, x_recv.at[group], device_id=(grp, ahead(off)), device_id_type=MESH
            ).start()
            return carry

        return body

    def send_label(offset, group):
        def body(i, carry):
            off = offset(i)
            spot = spot_of(off)
            pltpu.make_async_remote_copy(
                lab_s.at[spot], lab_r.at[spot], lab_send, lab_recv.at[group], device_id=(grp, ahead(off)), device_id_type=MESH
            ).start()
            return carry

        return body

    pl.semaphore_wait(barrier, near - 1 + 1 + chips - 1)
    for end in (REACH, zs - REACH):
        pl.semaphore_signal(near_sem, inc=1, device_id=(grp, lax.rem(z + end, zs) * YS + y), device_id_type=MESH)
    lax.fori_loop(0, near - 1, send_x(near_offset, 0), 0)
    lax.fori_loop(0, near - 1, send_label(near_offset, 0), 0)
    pl.semaphore_wait(near_sem, 2)
    lax.fori_loop(0, far, send_x(far_offset, 1), 0)
    lax.fori_loop(0, far, send_label(far_offset, 1), 0)
    x_ref[turn] = out_x[turn]
    lab_r[turn] = lab_s[turn]

    def bulk(src, dst, count, send, recv):
        return pltpu.make_async_remote_copy(
            src.at[pl.ds(0, count)], dst.at[pl.ds(0, count)], send, recv, device_id=partner, device_id_type=MESH
        )

    for load in loads:
        load.wait()

    task_row = lax.div(iota((2 * LANES, 1), 0), LANES)
    gate_w = gate_ref[...].astype(jnp.float32)
    gate_b = jnp.where(task_row == 0, gate_w[0:1], gate_w[1:2]).astype(jnp.bfloat16)
    tout_w = tout_ref[...].astype(jnp.float32)
    tout = jnp.concatenate([tout_w[0:1], tout_w[1:2]], axis=1)
    same_task = lax.div(iota((2 * LANES, 2 * LANES), 0), LANES) == lax.div(iota((2 * LANES, 2 * LANES), 1), LANES)
    tout_b = jnp.where(same_task, tout, 0.0).astype(jnp.bfloat16)

    def own_lane(blocks):
        lane = iota((blocks * CAP, LANES), 1)
        return lane, lax.rem(iota((blocks * CAP, LANES), 0), CAP) == lax.div(lane, 2)

    def forward(first, blocks):
        x = x_ref[pl.ds(first, blocks)].reshape(blocks * CAP, width)
        block = blocks * CAP
        acc = None
        for c in range(CHUNKS):
            at = pl.ds(c * cols, cols)
            h = jnp.maximum(dot(x, w_ref[:, at]), 0.0).astype(jnp.bfloat16)
            s = jnp.maximum(dot(x, s_ref[:, at]), 0.0).astype(jnp.bfloat16)
            hidden[pl.ds(first * CAP, block), at] = h
            more = dot(jnp.concatenate([h, s], axis=0), t_ref[at, :])
            acc = more if acc is None else acc + more
        gate = jax.nn.sigmoid(dot(x, gate_b, ((1,), (1,))))
        tower_in = gate * acc[:block] + (1.0 - gate) * acc[block:]
        act = jnp.maximum(tower_in, 0.0).astype(jnp.bfloat16)
        logit = dot(act, tout_b, ((1,), (1,)))
        lane, mine = own_lane(blocks)
        pick = jnp.where(lax.rem(lane, 2) == 0, logit[:, :LANES], logit[:, LANES:])
        lg_s[pl.ds(first, blocks)] = jnp.sum(
            jnp.where(mine, pick, 0.0).reshape(blocks, CAP, LANES), axis=1, keepdims=True
        )
        return gate, tower_in, logit

    def send_logit(offset):
        def body(i, carry):
            off = offset(i)
            spot = spot_of(off)
            pltpu.make_async_remote_copy(
                lg_s.at[spot], lg_r.at[spot], lg_send, lg_recv, device_id=(grp, behind(off)), device_id_type=MESH
            ).start()
            return carry

        return body

    fan = (lax.rem(iota((LANES, 2 * LANES), 0), 2) == lax.div(iota((LANES, 2 * LANES), 1), LANES)).astype(jnp.float32).astype(jnp.bfloat16)
    weight = 64.0 / jnp.sqrt(jnp.full((1, 2 * LANES), counts_ref[own], jnp.int32).astype(jnp.float32))
    d_new = iota((width, width), 0)
    d_old = iota((width, width), 1)
    from_row = (2 * lax.rem(lax.div(d_new, part), chips) + lax.div(d_new, part * chips)) * part + lax.rem(d_new, part)
    order = (d_old == from_row).astype(jnp.float32).astype(jnp.bfloat16)

    def gradient(first, blocks, side):
        gate, tower_in, logit = side
        block = blocks * CAP
        spread = (lax.div(iota((block, blocks), 0), CAP) == iota((block, blocks), 1)).astype(jnp.float32).astype(jnp.bfloat16)
        packed = dot(spread, lab_r[pl.ds(first, blocks)].reshape(blocks, LANES).astype(jnp.bfloat16))
        packed = jnp.where(own_lane(blocks)[1], packed, 0.0).astype(jnp.bfloat16)
        dlogit = weight * (jax.nn.sigmoid(logit) - dot(packed, fan))
        mixed = jnp.where(tower_in > 0.0, gate * dlogit * tout, 0.0).astype(jnp.bfloat16)
        x = x_ref[pl.ds(first, blocks)].reshape(block, width)
        return mixed, dot(order, x, ((1,), (1,))).astype(jnp.bfloat16)

    def share(first, blocks, mixed, x_t, c):
        at = pl.ds(c * cols, cols)
        back = dot(mixed, t_ref[at, :], ((1,), (1,))).astype(jnp.bfloat16)
        masked = jnp.where(hidden[pl.ds(first * CAP, blocks * CAP), at] > 0.0, back, jnp.zeros_like(back))
        return dot(x_t, masked).reshape(2, width // 2, cols)

    def core_copy(c):
        return pltpu.make_async_remote_copy(
            core_s.at[c, 1 - core], core_r.at[c], core_send.at[c], core_recv.at[c], device_id=partner, device_id_type=MESH
        )

    def link_copy(src, dst, send, recv, c, way):
        to = lax.rem(chip + (1, chips - 1)[way], chips)
        return pltpu.make_async_remote_copy(
            src.at[c, way],
            dst.at[c, way],
            send.at[c, way],
            recv.at[c, way],
            device_id=(2 * to + core, own),
            device_id_type=MESH,
        )

    def first_leg(c, way):
        return link_copy(link_s, link_r, link_send, link_recv, c, way)

    def second_leg(c, way):
        return link_copy(sum_s, sum_r, sum_send, sum_recv, c, way)

    bulk(out_x, x_ref, near - 1, x_send, x_recv.at[0]).wait_recv()
    near_side = forward(0, near)
    lax.fori_loop(0, near - 1, send_logit(near_offset), 0)
    lg_r[turn] = lg_s[turn]
    bulk(lab_s, lab_r, near - 1, lab_send, lab_recv.at[0]).wait_recv()
    mixed, x_t = gradient(0, near, near_side)
    for c in range(CHUNKS):
        core_f[c] = share(0, near, mixed, x_t, c)
    bulk(out_x, x_ref, far, x_send, x_recv.at[1]).wait_recv()
    far_side = forward(near, far)
    lax.fori_loop(0, far, send_logit(far_offset), 0)
    bulk(lab_s, lab_r, far, lab_send, lab_recv.at[1]).wait_recv()
    mixed, x_t = gradient(near, far, far_side)
    for c in range(CHUNKS):
        total = core_f[c] + share(near, far, mixed, x_t, c)
        core_f[c] = total
        core_s[c] = total.astype(jnp.bfloat16)
        core_copy(c).start()

    after, opposite, prior = (lax.rem(chip + d, chips) for d in (1, 2, 3))
    side = cols // 2
    for c in range(CHUNKS):
        core_copy(c).wait_recv()
        proj[c] = (core_f[c, core] + core_r[c].astype(jnp.float32)).reshape(chips, part, cols)
        link_s[c, 0, 0] = proj[c, opposite, :, pl.ds(0, side)].astype(jnp.bfloat16)
        link_s[c, 0, 1] = proj[c, after, :, pl.ds(side, side)].astype(jnp.bfloat16)
        first_leg(c, 0).start()
        link_s[c, 1, 0] = proj[c, opposite, :, pl.ds(side, side)].astype(jnp.bfloat16)
        link_s[c, 1, 1] = proj[c, prior, :, pl.ds(0, side)].astype(jnp.bfloat16)
        first_leg(c, 1).start()
    for c in range(CHUNKS):
        first_leg(c, 0).wait_recv()
        sum_s[c, 0] = (proj[c, after, :, pl.ds(0, side)] + link_r[c, 0, 0].astype(jnp.float32)).astype(jnp.bfloat16)
        second_leg(c, 0).start()
        first_leg(c, 1).wait_recv()
        sum_s[c, 1] = (proj[c, prior, :, pl.ds(side, side)] + link_r[c, 1, 0].astype(jnp.float32)).astype(jnp.bfloat16)
        second_leg(c, 1).start()
    for c in range(CHUNKS):
        for way in range(2):
            second_leg(c, way).wait_recv()
            total = proj[c, chip, :, pl.ds(way * side, side)] + link_r[c, 1 - way, 1].astype(jnp.float32)
            grad_ref[0, :, pl.ds(c * cols + way * side, side)] = total + sum_r[c, way].astype(jnp.float32)

    bulk(lg_s, lg_r, owners - 1, lg_send, lg_recv).wait_recv()
    got = lg_r[...].reshape(owners, LANES)
    found = dot(got, member.astype(jnp.float32), ((0,), (0,)), lax.Precision.HIGHEST)
    for task in range(2):
        logits_ref[pl.ds(task, 1), :] = jnp.sum(jnp.where(lane_t == 2 * rank + task, found, 0.0), axis=0, keepdims=True)

    bulk(out_x, x_ref, owners - 1, x_send, x_recv.at[0]).wait_send()
    bulk(lab_s, lab_r, owners - 1, lab_send, lab_recv.at[0]).wait_send()
    bulk(lg_s, lg_r, owners - 1, lg_send, lg_recv).wait_send()
    for c in range(CHUNKS):
        core_copy(c).wait_send()
        for way in range(2):
            first_leg(c, way).wait_send()
            second_leg(c, way).wait_send()


def shards(owners, groups, features, scenario_ids, labels, counts, scenario_weights, shared_weights, gate_weights, tower_weights, tower_out):
    tokens, width = features.shape
    expert, towers = tower_weights.shape
    cols = expert // CHUNKS
    part = width // groups
    chips = groups // 2
    vmem = pl.BlockSpec(memory_space=pltpu.VMEM)
    hbm = pl.BlockSpec(memory_space=pl.ANY)
    dma = pltpu.SemaphoreType.DMA
    bf16, f32 = jnp.bfloat16, jnp.float32
    return pl.pallas_call(
        functools.partial(step_kernel, owners, groups),
        out_shape=(pltpu.VMEM((2, tokens), f32), pltpu.VMEM((1, part, expert), f32)),
        in_specs=[vmem, vmem, vmem, pl.BlockSpec(memory_space=pltpu.SMEM), hbm, hbm, vmem, hbm, vmem],
        out_specs=(vmem, vmem),
        scratch_shapes=[
            pltpu.VMEM((width, expert), bf16),
            pltpu.VMEM((width, expert), bf16),
            pltpu.VMEM((expert, towers), bf16),
            pltpu.VMEM((owners, CAP, width), bf16),
            pltpu.VMEM((owners, CAP, width), bf16),
            pltpu.VMEM((owners, 1, LANES), f32),
            pltpu.VMEM((owners, 1, LANES), f32),
            pltpu.VMEM((owners, 1, LANES), f32),
            pltpu.VMEM((owners, 1, LANES), f32),
            pltpu.VMEM((owners * CAP, expert), bf16),
            pltpu.VMEM((CHUNKS, chips, part, cols), f32),
            pltpu.VMEM((CHUNKS, 2, width // 2, cols), bf16),
            pltpu.VMEM((CHUNKS, width // 2, cols), bf16),
            pltpu.VMEM((CHUNKS, 2, width // 2, cols), f32),
            pltpu.VMEM((CHUNKS, 2, 2, part, cols // 2), bf16),
            pltpu.VMEM((CHUNKS, 2, 2, part, cols // 2), bf16),
            pltpu.VMEM((CHUNKS, 2, part, cols // 2), bf16),
            pltpu.VMEM((CHUNKS, 2, part, cols // 2), bf16),
            dma((3,)),
            dma(()),
            dma((2,)),
            dma(()),
            dma((2,)),
            dma(()),
            dma(()),
            pltpu.SemaphoreType.REGULAR,
            dma((CHUNKS,)),
            dma((CHUNKS,)),
            dma((CHUNKS, 2)),
            dma((CHUNKS, 2)),
            dma((CHUNKS, 2)),
            dma((CHUNKS, 2)),
        ],
        compiler_params=pltpu.CompilerParams(collective_id=0, has_side_effects=True, vmem_limit_bytes=56 * 1024 * 1024),
    )(
        scenario_ids.reshape(1, tokens),
        labels,
        features,
        counts,
        scenario_weights,
        shared_weights,
        gate_weights.T,
        tower_weights,
        tower_out.reshape(2, towers // 2),
    )


def solution(mesh):
    return jax.shard_map(
        functools.partial(shards, mesh.shape["own"], mesh.shape["grp"]),
        mesh=mesh,
        in_specs=(
            P(("grp", "own"), None),
            P(("grp", "own")),
            P(None, ("grp", "own")),
            P(),
            P("own", None, None),
            P(),
            P(),
            P(),
            P(),
        ),
        out_specs=(P(None, ("grp", "own")), P("own", "grp", None)),
        check_vma=False,
    )
```

```python
import functools

import jax
import jax.numpy as jnp
from jax import lax
from jax.experimental import pallas as pl
from jax.experimental.pallas import tpu as pltpu
from jax.sharding import PartitionSpec as P

MESH = pl.DeviceIdType.MESH
CAP = 8
YS = 4
REACH = 4
LANES = 128
CHUNKS = 4


def dot(a, b, dims=((1,), (0,)), precision=None):
    return lax.dot_general(a, b, (dims, ((), ())), precision=precision, preferred_element_type=jnp.float32)


def iota(shape, dim):
    return lax.broadcasted_iota(jnp.int32, shape, dim)


def step_kernel(
    owners,
    groups,
    ids_hbm,
    labels_hbm,
    feats_hbm,
    counts_hbm,
    w_hbm,
    s_hbm,
    gate_hbm,
    t_hbm,
    tout_hbm,
    logits_ref,
    grad_ref,
    ids_ref,
    labels_ref,
    feats_ref,
    counts_ref,
    gate_ref,
    tout_ref,
    w_ref,
    s_ref,
    t_ref,
    out_x,
    x_ref,
    lab_s,
    lab_r,
    lg_s,
    lg_r,
    hidden,
    proj,
    core_s,
    core_r,
    core_f,
    link_s,
    link_r,
    sum_s,
    sum_r,
    load_sem,
    x_send,
    x_recv,
    lab_send,
    lab_recv,
    lg_send,
    lg_recv,
    near_sem,
    core_send,
    core_recv,
    link_send,
    link_recv,
    sum_send,
    sum_recv,
):
    own = lax.axis_index("own")
    grp = lax.axis_index("grp")
    core = lax.rem(grp, 2)
    chip = lax.div(grp, 2)
    chips = groups // 2
    partner = (grp + 1 - 2 * core, own)
    zs = owners // YS
    z = lax.div(own, YS)
    y = lax.rem(own, YS)
    turn = REACH * YS
    near = 2 * turn + YS
    far = owners - near
    tokens, width = feats_hbm.shape
    expert = w_ref.shape[1]
    cols = expert // CHUNKS
    rows = owners * CAP
    part = width // groups

    barrier = pltpu.get_barrier_semaphore()

    def near_offset(i):
        k = lax.div(i, 2)
        off = jnp.where(lax.rem(i, 2) == 0, turn + YS - 1 - k, owners - turn + k)
        return jnp.where(off == owners, 1, off)

    def far_offset(i):
        k = lax.div(i, 2)
        return jnp.where(lax.rem(i, 2) == 0, turn + YS + far // 2 - 1 - k, turn + YS + far // 2 + k)

    def spot_of(off):
        return lax.rem(off + turn, owners)

    def ahead(off):
        return lax.rem(z + lax.div(off, YS), zs) * YS + lax.rem(y + lax.rem(off, YS), YS)

    def behind(off):
        return lax.rem(z + zs - lax.div(off, YS), zs) * YS + lax.rem(y + YS - lax.rem(off, YS), YS)

    def greet(i, carry):
        pl.semaphore_signal(barrier, inc=1, device_id=(grp, ahead(near_offset(i))), device_id_type=MESH)
        return carry

    lax.fori_loop(0, near - 1, greet, 0)
    pl.semaphore_signal(barrier, inc=1, device_id=partner, device_id_type=MESH)
    for d in range(1, chips):
        pl.semaphore_signal(barrier, inc=1, device_id=(lax.rem(grp + 2 * d, groups), own), device_id_type=MESH)

    loads = [
        pltpu.make_async_copy(w_hbm.at[0], w_ref, load_sem.at[0]),
        pltpu.make_async_copy(s_hbm, s_ref, load_sem.at[1]),
        pltpu.make_async_copy(t_hbm, t_ref, load_sem.at[2]),
        pltpu.make_async_copy(counts_hbm, counts_ref, load_sem.at[3]),
        pltpu.make_async_copy(gate_hbm, gate_ref, load_sem.at[4]),
        pltpu.make_async_copy(tout_hbm, tout_ref, load_sem.at[5]),
    ]
    firsts = [
        pltpu.make_async_copy(ids_hbm, ids_ref, load_sem.at[6]),
        pltpu.make_async_copy(labels_hbm, labels_ref, load_sem.at[7]),
        pltpu.make_async_copy(feats_hbm, feats_ref, load_sem.at[8]),
    ]
    for load in firsts + loads:
        load.start()
    for load in firsts:
        load.wait()

    ids = ids_ref[...]
    to_z = lax.rem(lax.div(ids, YS) - z + zs, zs)
    to_y = lax.rem(lax.rem(ids, YS) - y + YS, YS)
    spots = spot_of(to_z * YS + to_y)
    member = iota((owners, tokens), 0) == spots
    member_b = member.astype(jnp.float32).astype(jnp.bfloat16)
    before = (iota((tokens, tokens), 0) < iota((tokens, tokens), 1)).astype(jnp.float32).astype(jnp.bfloat16)
    earlier = dot(member_b, before)
    rank = jnp.sum(jnp.where(member, earlier, 0.0), axis=0, keepdims=True).astype(jnp.int32)
    slot = spots * CAP + rank
    place = (iota((rows, tokens), 0) == slot).astype(jnp.float32).astype(jnp.bfloat16)
    out_x[...] = dot(place, feats_ref[...]).astype(jnp.bfloat16).reshape(owners, CAP, width)
    lane_t = iota((LANES, tokens), 0)
    labels_f = labels_ref[...].astype(jnp.float32)
    label_of = jnp.where(lax.rem(lane_t, 2) == 0, labels_f[0:1], labels_f[1:2])
    label_at = jnp.where(lax.div(lane_t, 2) == rank, label_of, 0.0).astype(jnp.bfloat16)
    lab_s[...] = dot(member_b, label_at, ((1,), (1,))).reshape(owners, 1, LANES)

    def send_x(offset, group):
        def body(i, carry):
            off = offset(i)
            spot = spot_of(off)
            pltpu.make_async_remote_copy(
                out_x.at[spot], x_ref.at[spot], x_send, x_recv.at[group], device_id=(grp, ahead(off)), device_id_type=MESH
            ).start()
            return carry

        return body

    def send_label(offset, group):
        def body(i, carry):
            off = offset(i)
            spot = spot_of(off)
            pltpu.make_async_remote_copy(
                lab_s.at[spot], lab_r.at[spot], lab_send, lab_recv.at[group], device_id=(grp, ahead(off)), device_id_type=MESH
            ).start()
            return carry

        return body

    pl.semaphore_wait(barrier, near - 1 + 1 + chips - 1)
    for end in (REACH, zs - REACH):
        pl.semaphore_signal(near_sem, inc=1, device_id=(grp, lax.rem(z + end, zs) * YS + y), device_id_type=MESH)
    lax.fori_loop(0, near - 1, send_x(near_offset, 0), 0)
    lax.fori_loop(0, near - 1, send_label(near_offset, 0), 0)
    pl.semaphore_wait(near_sem, 2)
    lax.fori_loop(0, far, send_x(far_offset, 1), 0)
    lax.fori_loop(0, far, send_label(far_offset, 1), 0)
    x_ref[turn] = out_x[turn]
    lab_r[turn] = lab_s[turn]

    def bulk(src, dst, count, send, recv):
        return pltpu.make_async_remote_copy(
            src.at[pl.ds(0, count)], dst.at[pl.ds(0, count)], send, recv, device_id=partner, device_id_type=MESH
        )

    for load in loads:
        load.wait()

    task_row = lax.div(iota((2 * LANES, 1), 0), LANES)
    gate_w = gate_ref[...].astype(jnp.float32)
    gate_b = jnp.where(task_row == 0, gate_w[0:1], gate_w[1:2]).astype(jnp.bfloat16)
    tout_w = tout_ref[...].astype(jnp.float32)
    tout = jnp.concatenate([tout_w[0:1], tout_w[1:2]], axis=1)
    same_task = lax.div(iota((2 * LANES, 2 * LANES), 0), LANES) == lax.div(iota((2 * LANES, 2 * LANES), 1), LANES)
    tout_b = jnp.where(same_task, tout, 0.0).astype(jnp.bfloat16)

    def own_lane(blocks):
        lane = iota((blocks * CAP, LANES), 1)
        return lane, lax.rem(iota((blocks * CAP, LANES), 0), CAP) == lax.div(lane, 2)

    def forward(first, blocks):
        x = x_ref[pl.ds(first, blocks)].reshape(blocks * CAP, width)
        block = blocks * CAP
        acc = None
        for c in range(CHUNKS):
            at = pl.ds(c * cols, cols)
            h = jnp.maximum(dot(x, w_ref[:, at]), 0.0).astype(jnp.bfloat16)
            s = jnp.maximum(dot(x, s_ref[:, at]), 0.0).astype(jnp.bfloat16)
            hidden[pl.ds(first * CAP, block), at] = h
            more = dot(jnp.concatenate([h, s], axis=0), t_ref[at, :])
            acc = more if acc is None else acc + more
        gate = jax.nn.sigmoid(dot(x, gate_b, ((1,), (1,))))
        tower_in = gate * acc[:block] + (1.0 - gate) * acc[block:]
        act = jnp.maximum(tower_in, 0.0).astype(jnp.bfloat16)
        logit = dot(act, tout_b, ((1,), (1,)))
        lane, mine = own_lane(blocks)
        pick = jnp.where(lax.rem(lane, 2) == 0, logit[:, :LANES], logit[:, LANES:])
        lg_s[pl.ds(first, blocks)] = jnp.sum(
            jnp.where(mine, pick, 0.0).reshape(blocks, CAP, LANES), axis=1, keepdims=True
        )
        return gate, tower_in, logit

    def send_logit(offset):
        def body(i, carry):
            off = offset(i)
            spot = spot_of(off)
            pltpu.make_async_remote_copy(
                lg_s.at[spot], lg_r.at[spot], lg_send, lg_recv, device_id=(grp, behind(off)), device_id_type=MESH
            ).start()
            return carry

        return body

    fan = (lax.rem(iota((LANES, 2 * LANES), 0), 2) == lax.div(iota((LANES, 2 * LANES), 1), LANES)).astype(jnp.float32).astype(jnp.bfloat16)
    weight = 64.0 / jnp.sqrt(jnp.full((1, 2 * LANES), counts_ref[own], jnp.int32).astype(jnp.float32))
    d_new = iota((width, width), 0)
    d_old = iota((width, width), 1)
    from_row = (2 * lax.rem(lax.div(d_new, part), chips) + lax.div(d_new, part * chips)) * part + lax.rem(d_new, part)
    order = (d_old == from_row).astype(jnp.float32).astype(jnp.bfloat16)

    def gradient(first, blocks, side):
        gate, tower_in, logit = side
        block = blocks * CAP
        spread = (lax.div(iota((block, blocks), 0), CAP) == iota((block, blocks), 1)).astype(jnp.float32).astype(jnp.bfloat16)
        packed = dot(spread, lab_r[pl.ds(first, blocks)].reshape(blocks, LANES).astype(jnp.bfloat16))
        packed = jnp.where(own_lane(blocks)[1], packed, 0.0).astype(jnp.bfloat16)
        dlogit = weight * (jax.nn.sigmoid(logit) - dot(packed, fan))
        mixed = jnp.where(tower_in > 0.0, gate * dlogit * tout, 0.0).astype(jnp.bfloat16)
        x = x_ref[pl.ds(first, blocks)].reshape(block, width)
        return mixed, dot(order, x, ((1,), (1,))).astype(jnp.bfloat16)

    def share(first, blocks, mixed, x_t, c):
        at = pl.ds(c * cols, cols)
        back = dot(mixed, t_ref[at, :], ((1,), (1,))).astype(jnp.bfloat16)
        masked = jnp.where(hidden[pl.ds(first * CAP, blocks * CAP), at] > 0.0, back, jnp.zeros_like(back))
        return dot(x_t, masked).reshape(2, width // 2, cols)

    def core_copy(c):
        return pltpu.make_async_remote_copy(
            core_s.at[c, 1 - core], core_r.at[c], core_send.at[c], core_recv.at[c], device_id=partner, device_id_type=MESH
        )

    def link_copy(src, dst, send, recv, c, way):
        to = lax.rem(chip + (1, chips - 1)[way], chips)
        return pltpu.make_async_remote_copy(
            src.at[c, way],
            dst.at[c, way],
            send.at[c, way],
            recv.at[c, way],
            device_id=(2 * to + core, own),
            device_id_type=MESH,
        )

    def first_leg(c, way):
        return link_copy(link_s, link_r, link_send, link_recv, c, way)

    def second_leg(c, way):
        return link_copy(sum_s, sum_r, sum_send, sum_recv, c, way)

    bulk(out_x, x_ref, near - 1, x_send, x_recv.at[0]).wait_recv()
    near_side = forward(0, near)
    lax.fori_loop(0, near - 1, send_logit(near_offset), 0)
    lg_r[turn] = lg_s[turn]
    bulk(lab_s, lab_r, near - 1, lab_send, lab_recv.at[0]).wait_recv()
    mixed, x_t = gradient(0, near, near_side)
    for c in range(CHUNKS):
        core_f[c] = share(0, near, mixed, x_t, c)
    bulk(out_x, x_ref, far, x_send, x_recv.at[1]).wait_recv()
    far_side = forward(near, far)
    bulk(lab_s, lab_r, far, lab_send, lab_recv.at[1]).wait_recv()
    mixed, x_t = gradient(near, far, far_side)
    for c in range(CHUNKS):
        total = core_f[c] + share(near, far, mixed, x_t, c)
        core_f[c] = total
        core_s[c] = total.astype(jnp.bfloat16)
        core_copy(c).start()
    lax.fori_loop(0, far, send_logit(far_offset), 0)

    after, opposite, prior = (lax.rem(chip + d, chips) for d in (1, 2, 3))
    side = cols // 2
    for c in range(CHUNKS):
        core_copy(c).wait_recv()
        proj[c] = (core_f[c, core] + core_r[c].astype(jnp.float32)).reshape(chips, part, cols)
        link_s[c, 0, 0] = proj[c, opposite, :, pl.ds(0, side)].astype(jnp.bfloat16)
        link_s[c, 0, 1] = proj[c, after, :, pl.ds(side, side)].astype(jnp.bfloat16)
        first_leg(c, 0).start()
        link_s[c, 1, 0] = proj[c, opposite, :, pl.ds(side, side)].astype(jnp.bfloat16)
        link_s[c, 1, 1] = proj[c, prior, :, pl.ds(0, side)].astype(jnp.bfloat16)
        first_leg(c, 1).start()
    for c in range(CHUNKS):
        first_leg(c, 0).wait_recv()
        sum_s[c, 0] = (proj[c, after, :, pl.ds(0, side)] + link_r[c, 0, 0].astype(jnp.float32)).astype(jnp.bfloat16)
        second_leg(c, 0).start()
        first_leg(c, 1).wait_recv()
        sum_s[c, 1] = (proj[c, prior, :, pl.ds(side, side)] + link_r[c, 1, 0].astype(jnp.float32)).astype(jnp.bfloat16)
        second_leg(c, 1).start()
    bulk(lg_s, lg_r, owners - 1, lg_send, lg_recv).wait_recv()
    got = lg_r[...].reshape(owners, LANES)
    found = dot(got, member.astype(jnp.float32), ((0,), (0,)), lax.Precision.HIGHEST)
    for task in range(2):
        logits_ref[pl.ds(task, 1), :] = jnp.sum(jnp.where(lane_t == 2 * rank + task, found, 0.0), axis=0, keepdims=True)

    for c in range(CHUNKS):
        for way in range(2):
            second_leg(c, way).wait_recv()
            total = proj[c, chip, :, pl.ds(way * side, side)] + link_r[c, 1 - way, 1].astype(jnp.float32)
            grad_ref[0, :, pl.ds(c * cols + way * side, side)] = total + sum_r[c, way].astype(jnp.float32)

    bulk(out_x, x_ref, owners - 1, x_send, x_recv.at[0]).wait_send()
    bulk(lab_s, lab_r, owners - 1, lab_send, lab_recv.at[0]).wait_send()
    bulk(lg_s, lg_r, owners - 1, lg_send, lg_recv).wait_send()
    for c in range(CHUNKS):
        core_copy(c).wait_send()
        for way in range(2):
            first_leg(c, way).wait_send()
            second_leg(c, way).wait_send()


def shards(owners, groups, features, scenario_ids, labels, counts, scenario_weights, shared_weights, gate_weights, tower_weights, tower_out):
    tokens, width = features.shape
    expert, towers = tower_weights.shape
    cols = expert // CHUNKS
    part = width // groups
    chips = groups // 2
    vmem = pl.BlockSpec(memory_space=pltpu.VMEM)
    hbm = pl.BlockSpec(memory_space=pltpu.HBM)
    dma = pltpu.SemaphoreType.DMA
    bf16, f32 = jnp.bfloat16, jnp.float32
    return pl.pallas_call(
        functools.partial(step_kernel, owners, groups),
        out_shape=(pltpu.VMEM((2, tokens), f32), pltpu.VMEM((1, part, expert), f32)),
        in_specs=[hbm] * 9,
        out_specs=(vmem, vmem),
        scratch_shapes=[
            pltpu.VMEM((1, tokens), jnp.int32),
            pltpu.VMEM((2, tokens), jnp.int32),
            pltpu.VMEM((tokens, width), bf16),
            pltpu.SMEM((owners,), jnp.int32),
            pltpu.VMEM((2, width), bf16),
            pltpu.VMEM((2, towers // 2), bf16),
            pltpu.VMEM((width, expert), bf16),
            pltpu.VMEM((width, expert), bf16),
            pltpu.VMEM((expert, towers), bf16),
            pltpu.VMEM((owners, CAP, width), bf16),
            pltpu.VMEM((owners, CAP, width), bf16),
            pltpu.VMEM((owners, 1, LANES), f32),
            pltpu.VMEM((owners, 1, LANES), f32),
            pltpu.VMEM((owners, 1, LANES), f32),
            pltpu.VMEM((owners, 1, LANES), f32),
            pltpu.VMEM((owners * CAP, expert), bf16),
            pltpu.VMEM((CHUNKS, chips, part, cols), f32),
            pltpu.VMEM((CHUNKS, 2, width // 2, cols), bf16),
            pltpu.VMEM((CHUNKS, width // 2, cols), bf16),
            pltpu.VMEM((CHUNKS, 2, width // 2, cols), f32),
            pltpu.VMEM((CHUNKS, 2, 2, part, cols // 2), bf16),
            pltpu.VMEM((CHUNKS, 2, 2, part, cols // 2), bf16),
            pltpu.VMEM((CHUNKS, 2, part, cols // 2), bf16),
            pltpu.VMEM((CHUNKS, 2, part, cols // 2), bf16),
            dma((9,)),
            dma(()),
            dma((2,)),
            dma(()),
            dma((2,)),
            dma(()),
            dma(()),
            pltpu.SemaphoreType.REGULAR,
            dma((CHUNKS,)),
            dma((CHUNKS,)),
            dma((CHUNKS, 2)),
            dma((CHUNKS, 2)),
            dma((CHUNKS, 2)),
            dma((CHUNKS, 2)),
        ],
        compiler_params=pltpu.CompilerParams(collective_id=0, has_side_effects=True, vmem_limit_bytes=56 * 1024 * 1024),
    )(
        scenario_ids.reshape(1, tokens),
        labels,
        features,
        counts,
        scenario_weights,
        shared_weights,
        gate_weights.T,
        tower_weights,
        tower_out.reshape(2, towers // 2),
    )


def solution(mesh):
    return jax.shard_map(
        functools.partial(shards, mesh.shape["own"], mesh.shape["grp"]),
        mesh=mesh,
        in_specs=(
            P(("grp", "own"), None),
            P(("grp", "own")),
            P(None, ("grp", "own")),
            P(),
            P("own", None, None),
            P(),
            P(),
            P(),
            P(),
        ),
        out_specs=(P(None, ("grp", "own")), P("own", "grp", None)),
        check_vma=False,
    )
```

```python
import functools

import jax
import jax.numpy as jnp
from jax import lax
from jax.experimental import pallas as pl
from jax.experimental.pallas import tpu as pltpu
from jax.sharding import PartitionSpec as P

MESH = pl.DeviceIdType.MESH
CAP = 8
YS = 4
REACH = 4
LANES = 128
CHUNKS = 4


def dot(a, b, dims=((1,), (0,)), precision=None):
    return lax.dot_general(a, b, (dims, ((), ())), precision=precision, preferred_element_type=jnp.float32)


def iota(shape, dim):
    return lax.broadcasted_iota(jnp.int32, shape, dim)


def step_kernel(
    owners,
    groups,
    ids_hbm,
    labels_hbm,
    feats_hbm,
    counts_hbm,
    w_hbm,
    s_hbm,
    gate_hbm,
    t_hbm,
    tout_hbm,
    logits_ref,
    grad_ref,
    ids_ref,
    labels_ref,
    feats_ref,
    counts_ref,
    gate_ref,
    tout_ref,
    w_ref,
    s_ref,
    t_ref,
    out_x,
    x_ref,
    lab_s,
    lab_r,
    lg_s,
    lg_r,
    hidden,
    proj,
    core_s,
    core_r,
    core_f,
    link_s,
    link_r,
    sum_s,
    sum_r,
    load_sem,
    x_send,
    x_recv,
    lab_send,
    lab_recv,
    lg_send,
    lg_recv,
    near_sem,
    core_send,
    core_recv,
    link_send,
    link_recv,
    sum_send,
    sum_recv,
):
    own = lax.axis_index("own")
    grp = lax.axis_index("grp")
    core = lax.rem(grp, 2)
    chip = lax.div(grp, 2)
    chips = groups // 2
    partner = (grp + 1 - 2 * core, own)
    zs = owners // YS
    z = lax.div(own, YS)
    y = lax.rem(own, YS)
    turn = REACH * YS
    near = 2 * turn + YS
    far = owners - near
    tokens, width = feats_hbm.shape
    expert = w_ref.shape[1]
    cols = expert // CHUNKS
    rows = owners * CAP
    part = width // groups

    barrier = pltpu.get_barrier_semaphore()

    def near_offset(i):
        k = lax.div(i, 2)
        off = jnp.where(lax.rem(i, 2) == 0, turn + YS - 1 - k, owners - turn + k)
        return jnp.where(off == owners, 1, off)

    def far_offset(i):
        k = lax.div(i, 2)
        return jnp.where(lax.rem(i, 2) == 0, turn + YS + far // 2 - 1 - k, turn + YS + far // 2 + k)

    def spot_of(off):
        return lax.rem(off + turn, owners)

    def ahead(off):
        return lax.rem(z + lax.div(off, YS), zs) * YS + lax.rem(y + lax.rem(off, YS), YS)

    def behind(off):
        return lax.rem(z + zs - lax.div(off, YS), zs) * YS + lax.rem(y + YS - lax.rem(off, YS), YS)

    early_z = zs // 2
    early = z < early_z

    def greet(offset):
        def body(i, carry):
            pl.semaphore_signal(barrier, inc=1, device_id=(grp, ahead(offset(i))), device_id_type=MESH)
            return carry

        return body

    @pl.when(early)
    def _():
        lax.fori_loop(0, far, greet(far_offset), 0)

    lax.fori_loop(0, near - 1, greet(near_offset), 0)
    pl.semaphore_signal(barrier, inc=1, device_id=partner, device_id_type=MESH)
    for d in range(1, chips):
        pl.semaphore_signal(barrier, inc=1, device_id=(lax.rem(grp + 2 * d, groups), own), device_id_type=MESH)

    loads = [
        pltpu.make_async_copy(w_hbm.at[0], w_ref, load_sem.at[0]),
        pltpu.make_async_copy(s_hbm, s_ref, load_sem.at[1]),
        pltpu.make_async_copy(t_hbm, t_ref, load_sem.at[2]),
        pltpu.make_async_copy(counts_hbm, counts_ref, load_sem.at[3]),
        pltpu.make_async_copy(gate_hbm, gate_ref, load_sem.at[4]),
        pltpu.make_async_copy(tout_hbm, tout_ref, load_sem.at[5]),
    ]
    firsts = [
        pltpu.make_async_copy(ids_hbm, ids_ref, load_sem.at[6]),
        pltpu.make_async_copy(labels_hbm, labels_ref, load_sem.at[7]),
        pltpu.make_async_copy(feats_hbm, feats_ref, load_sem.at[8]),
    ]
    for load in firsts + loads:
        load.start()
    for load in firsts:
        load.wait()

    ids = ids_ref[...]
    to_z = lax.rem(lax.div(ids, YS) - z + zs, zs)
    to_y = lax.rem(lax.rem(ids, YS) - y + YS, YS)
    spots = spot_of(to_z * YS + to_y)
    member = iota((owners, tokens), 0) == spots
    member_b = member.astype(jnp.float32).astype(jnp.bfloat16)
    before = (iota((tokens, tokens), 0) < iota((tokens, tokens), 1)).astype(jnp.float32).astype(jnp.bfloat16)
    earlier = dot(member_b, before)
    rank = jnp.sum(jnp.where(member, earlier, 0.0), axis=0, keepdims=True).astype(jnp.int32)
    slot = spots * CAP + rank
    place = (iota((rows, tokens), 0) == slot).astype(jnp.float32).astype(jnp.bfloat16)
    out_x[...] = dot(place, feats_ref[...]).astype(jnp.bfloat16).reshape(owners, CAP, width)
    lane_t = iota((LANES, tokens), 0)
    labels_f = labels_ref[...].astype(jnp.float32)
    label_of = jnp.where(lax.rem(lane_t, 2) == 0, labels_f[0:1], labels_f[1:2])
    label_at = jnp.where(lax.div(lane_t, 2) == rank, label_of, 0.0).astype(jnp.bfloat16)
    lab_s[...] = dot(member_b, label_at, ((1,), (1,))).reshape(owners, 1, LANES)

    def send_x(offset, group):
        def body(i, carry):
            off = offset(i)
            spot = spot_of(off)
            pltpu.make_async_remote_copy(
                out_x.at[spot], x_ref.at[spot], x_send, x_recv.at[group], device_id=(grp, ahead(off)), device_id_type=MESH
            ).start()
            return carry

        return body

    def send_label(offset, group):
        def body(i, carry):
            off = offset(i)
            spot = spot_of(off)
            pltpu.make_async_remote_copy(
                lab_s.at[spot], lab_r.at[spot], lab_send, lab_recv.at[group], device_id=(grp, ahead(off)), device_id_type=MESH
            ).start()
            return carry

        return body

    def send_far(to_early):
        def body(i, carry):
            dest = lax.rem(z + lax.div(far_offset(i), YS), zs)

            @pl.when((dest < early_z) if to_early else (dest >= early_z))
            def _():
                send_x(far_offset, 1)(i, 0)

            return carry

        return body

    greeted = early_z * YS - jnp.where(early, 1, 0) + jnp.where(early, 0, YS - 1)
    for d in range(1, REACH + 1):
        for end in (d, zs - d):
            greeted = greeted + jnp.where(lax.rem(z + end, zs) < early_z, 0, YS)
    pl.semaphore_wait(barrier, greeted + 1 + chips - 1)
    for end in (REACH, zs - REACH):
        pl.semaphore_signal(near_sem, inc=1, device_id=(grp, lax.rem(z + end, zs) * YS + y), device_id_type=MESH)
    lax.fori_loop(0, far, send_far(True), 0)
    lax.fori_loop(0, near - 1, send_x(near_offset, 0), 0)
    lax.fori_loop(0, near - 1, send_label(near_offset, 0), 0)
    pl.semaphore_wait(near_sem, 2)
    lax.fori_loop(0, far, send_far(False), 0)
    lax.fori_loop(0, far, send_label(far_offset, 1), 0)
    x_ref[turn] = out_x[turn]
    lab_r[turn] = lab_s[turn]

    def bulk(src, dst, count, send, recv):
        return pltpu.make_async_remote_copy(
            src.at[pl.ds(0, count)], dst.at[pl.ds(0, count)], send, recv, device_id=partner, device_id_type=MESH
        )

    for load in loads:
        load.wait()

    task_row = lax.div(iota((2 * LANES, 1), 0), LANES)
    gate_w = gate_ref[...].astype(jnp.float32)
    gate_b = jnp.where(task_row == 0, gate_w[0:1], gate_w[1:2]).astype(jnp.bfloat16)
    tout_w = tout_ref[...].astype(jnp.float32)
    tout = jnp.concatenate([tout_w[0:1], tout_w[1:2]], axis=1)
    same_task = lax.div(iota((2 * LANES, 2 * LANES), 0), LANES) == lax.div(iota((2 * LANES, 2 * LANES), 1), LANES)
    tout_b = jnp.where(same_task, tout, 0.0).astype(jnp.bfloat16)

    def own_lane(blocks):
        lane = iota((blocks * CAP, LANES), 1)
        return lane, lax.rem(iota((blocks * CAP, LANES), 0), CAP) == lax.div(lane, 2)

    def forward(first, blocks):
        x = x_ref[pl.ds(first, blocks)].reshape(blocks * CAP, width)
        block = blocks * CAP
        acc = None
        for c in range(CHUNKS):
            at = pl.ds(c * cols, cols)
            h = jnp.maximum(dot(x, w_ref[:, at]), 0.0).astype(jnp.bfloat16)
            s = jnp.maximum(dot(x, s_ref[:, at]), 0.0).astype(jnp.bfloat16)
            hidden[pl.ds(first * CAP, block), at] = h
            more = dot(jnp.concatenate([h, s], axis=0), t_ref[at, :])
            acc = more if acc is None else acc + more
        gate = jax.nn.sigmoid(dot(x, gate_b, ((1,), (1,))))
        tower_in = gate * acc[:block] + (1.0 - gate) * acc[block:]
        act = jnp.maximum(tower_in, 0.0).astype(jnp.bfloat16)
        logit = dot(act, tout_b, ((1,), (1,)))
        lane, mine = own_lane(blocks)
        pick = jnp.where(lax.rem(lane, 2) == 0, logit[:, :LANES], logit[:, LANES:])
        lg_s[pl.ds(first, blocks)] = jnp.sum(
            jnp.where(mine, pick, 0.0).reshape(blocks, CAP, LANES), axis=1, keepdims=True
        )
        return gate, tower_in, logit

    def send_logit(offset):
        def body(i, carry):
            off = offset(i)
            spot = spot_of(off)
            pltpu.make_async_remote_copy(
                lg_s.at[spot], lg_r.at[spot], lg_send, lg_recv, device_id=(grp, behind(off)), device_id_type=MESH
            ).start()
            return carry

        return body

    fan = (lax.rem(iota((LANES, 2 * LANES), 0), 2) == lax.div(iota((LANES, 2 * LANES), 1), LANES)).astype(jnp.float32).astype(jnp.bfloat16)
    weight = 64.0 / jnp.sqrt(jnp.full((1, 2 * LANES), counts_ref[own], jnp.int32).astype(jnp.float32))
    d_new = iota((width, width), 0)
    d_old = iota((width, width), 1)
    from_row = (2 * lax.rem(lax.div(d_new, part), chips) + lax.div(d_new, part * chips)) * part + lax.rem(d_new, part)
    order = (d_old == from_row).astype(jnp.float32).astype(jnp.bfloat16)

    def gradient(first, blocks, side):
        gate, tower_in, logit = side
        block = blocks * CAP
        spread = (lax.div(iota((block, blocks), 0), CAP) == iota((block, blocks), 1)).astype(jnp.float32).astype(jnp.bfloat16)
        packed = dot(spread, lab_r[pl.ds(first, blocks)].reshape(blocks, LANES).astype(jnp.bfloat16))
        packed = jnp.where(own_lane(blocks)[1], packed, 0.0).astype(jnp.bfloat16)
        dlogit = weight * (jax.nn.sigmoid(logit) - dot(packed, fan))
        mixed = jnp.where(tower_in > 0.0, gate * dlogit * tout, 0.0).astype(jnp.bfloat16)
        x = x_ref[pl.ds(first, blocks)].reshape(block, width)
        return mixed, dot(order, x, ((1,), (1,))).astype(jnp.bfloat16)

    def share(first, blocks, mixed, x_t, c):
        at = pl.ds(c * cols, cols)
        back = dot(mixed, t_ref[at, :], ((1,), (1,))).astype(jnp.bfloat16)
        masked = jnp.where(hidden[pl.ds(first * CAP, blocks * CAP), at] > 0.0, back, jnp.zeros_like(back))
        return dot(x_t, masked).reshape(2, width // 2, cols)

    def core_copy(c):
        return pltpu.make_async_remote_copy(
            core_s.at[c, 1 - core], core_r.at[c], core_send.at[c], core_recv.at[c], device_id=partner, device_id_type=MESH
        )

    def link_copy(src, dst, send, recv, c, way):
        to = lax.rem(chip + (1, chips - 1)[way], chips)
        return pltpu.make_async_remote_copy(
            src.at[c, way],
            dst.at[c, way],
            send.at[c, way],
            recv.at[c, way],
            device_id=(2 * to + core, own),
            device_id_type=MESH,
        )

    def first_leg(c, way):
        return link_copy(link_s, link_r, link_send, link_recv, c, way)

    def second_leg(c, way):
        return link_copy(sum_s, sum_r, sum_send, sum_recv, c, way)

    bulk(out_x, x_ref, near - 1, x_send, x_recv.at[0]).wait_recv()
    near_side = forward(0, near)
    lax.fori_loop(0, near - 1, send_logit(near_offset), 0)
    lg_r[turn] = lg_s[turn]
    bulk(lab_s, lab_r, near - 1, lab_send, lab_recv.at[0]).wait_recv()
    mixed, x_t = gradient(0, near, near_side)
    for c in range(CHUNKS):
        core_f[c] = share(0, near, mixed, x_t, c)
    bulk(out_x, x_ref, far, x_send, x_recv.at[1]).wait_recv()
    far_side = forward(near, far)

    @pl.when(z >= early_z)
    def _():
        lax.fori_loop(0, far, send_logit(far_offset), 0)

    bulk(lab_s, lab_r, far, lab_send, lab_recv.at[1]).wait_recv()
    mixed, x_t = gradient(near, far, far_side)
    for c in range(CHUNKS):
        total = core_f[c] + share(near, far, mixed, x_t, c)
        core_f[c] = total
        core_s[c] = total.astype(jnp.bfloat16)
        core_copy(c).start()

    @pl.when(early)
    def _():
        lax.fori_loop(0, far, send_logit(far_offset), 0)

    after, opposite, prior = (lax.rem(chip + d, chips) for d in (1, 2, 3))
    side = cols // 2
    for c in range(CHUNKS):
        core_copy(c).wait_recv()
        proj[c] = (core_f[c, core] + core_r[c].astype(jnp.float32)).reshape(chips, part, cols)
        link_s[c, 0, 0] = proj[c, opposite, :, pl.ds(0, side)].astype(jnp.bfloat16)
        link_s[c, 0, 1] = proj[c, after, :, pl.ds(side, side)].astype(jnp.bfloat16)
        first_leg(c, 0).start()
        link_s[c, 1, 0] = proj[c, opposite, :, pl.ds(side, side)].astype(jnp.bfloat16)
        link_s[c, 1, 1] = proj[c, prior, :, pl.ds(0, side)].astype(jnp.bfloat16)
        first_leg(c, 1).start()
    for c in range(CHUNKS):
        first_leg(c, 0).wait_recv()
        sum_s[c, 0] = (proj[c, after, :, pl.ds(0, side)] + link_r[c, 0, 0].astype(jnp.float32)).astype(jnp.bfloat16)
        second_leg(c, 0).start()
        first_leg(c, 1).wait_recv()
        sum_s[c, 1] = (proj[c, prior, :, pl.ds(side, side)] + link_r[c, 1, 0].astype(jnp.float32)).astype(jnp.bfloat16)
        second_leg(c, 1).start()
    bulk(lg_s, lg_r, owners - 1, lg_send, lg_recv).wait_recv()
    got = lg_r[...].reshape(owners, LANES)
    found = dot(got, member.astype(jnp.float32), ((0,), (0,)), lax.Precision.HIGHEST)
    for task in range(2):
        logits_ref[pl.ds(task, 1), :] = jnp.sum(jnp.where(lane_t == 2 * rank + task, found, 0.0), axis=0, keepdims=True)

    for c in range(CHUNKS):
        for way in range(2):
            second_leg(c, way).wait_recv()
            total = proj[c, chip, :, pl.ds(way * side, side)] + link_r[c, 1 - way, 1].astype(jnp.float32)
            grad_ref[0, :, pl.ds(c * cols + way * side, side)] = total + sum_r[c, way].astype(jnp.float32)

    bulk(out_x, x_ref, owners - 1, x_send, x_recv.at[0]).wait_send()
    bulk(lab_s, lab_r, owners - 1, lab_send, lab_recv.at[0]).wait_send()
    bulk(lg_s, lg_r, owners - 1, lg_send, lg_recv).wait_send()
    for c in range(CHUNKS):
        core_copy(c).wait_send()
        for way in range(2):
            first_leg(c, way).wait_send()
            second_leg(c, way).wait_send()


def shards(owners, groups, features, scenario_ids, labels, counts, scenario_weights, shared_weights, gate_weights, tower_weights, tower_out):
    tokens, width = features.shape
    expert, towers = tower_weights.shape
    cols = expert // CHUNKS
    part = width // groups
    chips = groups // 2
    vmem = pl.BlockSpec(memory_space=pltpu.VMEM)
    hbm = pl.BlockSpec(memory_space=pltpu.HBM)
    dma = pltpu.SemaphoreType.DMA
    bf16, f32 = jnp.bfloat16, jnp.float32
    return pl.pallas_call(
        functools.partial(step_kernel, owners, groups),
        out_shape=(pltpu.VMEM((2, tokens), f32), pltpu.VMEM((1, part, expert), f32)),
        in_specs=[hbm] * 9,
        out_specs=(vmem, vmem),
        scratch_shapes=[
            pltpu.VMEM((1, tokens), jnp.int32),
            pltpu.VMEM((2, tokens), jnp.int32),
            pltpu.VMEM((tokens, width), bf16),
            pltpu.SMEM((owners,), jnp.int32),
            pltpu.VMEM((2, width), bf16),
            pltpu.VMEM((2, towers // 2), bf16),
            pltpu.VMEM((width, expert), bf16),
            pltpu.VMEM((width, expert), bf16),
            pltpu.VMEM((expert, towers), bf16),
            pltpu.VMEM((owners, CAP, width), bf16),
            pltpu.VMEM((owners, CAP, width), bf16),
            pltpu.VMEM((owners, 1, LANES), f32),
            pltpu.VMEM((owners, 1, LANES), f32),
            pltpu.VMEM((owners, 1, LANES), f32),
            pltpu.VMEM((owners, 1, LANES), f32),
            pltpu.VMEM((owners * CAP, expert), bf16),
            pltpu.VMEM((CHUNKS, chips, part, cols), f32),
            pltpu.VMEM((CHUNKS, 2, width // 2, cols), bf16),
            pltpu.VMEM((CHUNKS, width // 2, cols), bf16),
            pltpu.VMEM((CHUNKS, 2, width // 2, cols), f32),
            pltpu.VMEM((CHUNKS, 2, 2, part, cols // 2), bf16),
            pltpu.VMEM((CHUNKS, 2, 2, part, cols // 2), bf16),
            pltpu.VMEM((CHUNKS, 2, part, cols // 2), bf16),
            pltpu.VMEM((CHUNKS, 2, part, cols // 2), bf16),
            dma((9,)),
            dma(()),
            dma((2,)),
            dma(()),
            dma((2,)),
            dma(()),
            dma(()),
            pltpu.SemaphoreType.REGULAR,
            dma((CHUNKS,)),
            dma((CHUNKS,)),
            dma((CHUNKS, 2)),
            dma((CHUNKS, 2)),
            dma((CHUNKS, 2)),
            dma((CHUNKS, 2)),
        ],
        compiler_params=pltpu.CompilerParams(collective_id=0, has_side_effects=True, vmem_limit_bytes=56 * 1024 * 1024),
    )(
        scenario_ids.reshape(1, tokens),
        labels,
        features,
        counts,
        scenario_weights,
        shared_weights,
        gate_weights.T,
        tower_weights,
        tower_out.reshape(2, towers // 2),
    )


def solution(mesh):
    return jax.shard_map(
        functools.partial(shards, mesh.shape["own"], mesh.shape["grp"]),
        mesh=mesh,
        in_specs=(
            P(("grp", "own"), None),
            P(("grp", "own")),
            P(None, ("grp", "own")),
            P(),
            P("own", None, None),
            P(),
            P(),
            P(),
            P(),
        ),
        out_specs=(P(None, ("grp", "own")), P("own", "grp", None)),
        check_vma=False,
    )
```

```python
import functools

import jax
import jax.numpy as jnp
from jax import lax
from jax.experimental import pallas as pl
from jax.experimental.pallas import tpu as pltpu
from jax.sharding import PartitionSpec as P

MESH = pl.DeviceIdType.MESH
CAP = 8
YS = 4
REACH = 4
LANES = 128
CHUNKS = 4


def dot(a, b, dims=((1,), (0,)), precision=None):
    return lax.dot_general(a, b, (dims, ((), ())), precision=precision, preferred_element_type=jnp.float32)


def iota(shape, dim):
    return lax.broadcasted_iota(jnp.int32, shape, dim)


def step_kernel(
    owners,
    groups,
    ids_hbm,
    labels_hbm,
    feats_hbm,
    counts_hbm,
    w_hbm,
    s_hbm,
    gate_hbm,
    t_hbm,
    tout_hbm,
    logits_ref,
    grad_ref,
    ids_ref,
    labels_ref,
    feats_ref,
    counts_ref,
    gate_ref,
    tout_ref,
    w_ref,
    s_ref,
    t_ref,
    out_x,
    x_ref,
    lab_s,
    lab_r,
    lg_s,
    lg_r,
    hidden,
    proj,
    core_s,
    core_r,
    core_f,
    link_s,
    link_r,
    load_sem,
    x_send,
    x_recv,
    lab_send,
    lab_recv,
    lg_send,
    lg_recv,
    near_sem,
    core_send,
    core_recv,
    link_send,
    link_recv,
):
    own = lax.axis_index("own")
    grp = lax.axis_index("grp")
    core = lax.rem(grp, 2)
    chip = lax.div(grp, 2)
    chips = groups // 2
    partner = (grp + 1 - 2 * core, own)
    zs = owners // YS
    z = lax.div(own, YS)
    y = lax.rem(own, YS)
    turn = REACH * YS
    near = 2 * turn + YS
    far = owners - near
    tokens, width = feats_hbm.shape
    expert = w_ref.shape[1]
    cols = expert // CHUNKS
    rows = owners * CAP
    part = width // groups

    barrier = pltpu.get_barrier_semaphore()

    def wrap(v, n):
        return jnp.where(v < 0, v + n, jnp.where(v >= n, v - n, v))

    y_ahead = [wrap(y + d, YS) for d in range(YS)]
    y_behind = [wrap(y - d, YS) for d in range(YS)]

    def row(send, v, first=0, back=False):
        to_z = wrap(z - v if back else z + v, zs) * YS
        for d in range(first, YS):
            send(turn + YS * v + d, to_z + (y_behind if back else y_ahead)[d])

    def near_rows(send, back=False):
        def body(i, carry):
            row(send, REACH - i, back=back)
            row(send, i - REACH, back=back)
            return carry

        lax.fori_loop(0, REACH, body, 0)
        row(send, 0, 1, back)

    def far_rows(send, back=False):
        def one(v):
            row(send, v, back=back)

        def body(i, carry):
            one(zs // 2 - i)
            one(zs // 2 + i)
            return carry

        one(zs // 2)
        lax.fori_loop(1, zs // 2 - REACH, body, 0)

    def greet(spot, target):
        pl.semaphore_signal(barrier, inc=1, device_id=(grp, target), device_id_type=MESH)

    early_z = zs // 2
    early = z < early_z
    near_rows(greet)
    pl.semaphore_signal(barrier, inc=1, device_id=partner, device_id_type=MESH)
    for d in range(1, chips):
        pl.semaphore_signal(barrier, inc=1, device_id=(lax.rem(grp + 2 * d, groups), own), device_id_type=MESH)

    loads = [
        pltpu.make_async_copy(w_hbm.at[0], w_ref, load_sem.at[0]),
        pltpu.make_async_copy(s_hbm, s_ref, load_sem.at[1]),
        pltpu.make_async_copy(t_hbm, t_ref, load_sem.at[2]),
        pltpu.make_async_copy(counts_hbm, counts_ref, load_sem.at[3]),
        pltpu.make_async_copy(gate_hbm, gate_ref, load_sem.at[4]),
        pltpu.make_async_copy(tout_hbm, tout_ref, load_sem.at[5]),
    ]
    firsts = [
        pltpu.make_async_copy(ids_hbm, ids_ref, load_sem.at[6]),
        pltpu.make_async_copy(labels_hbm, labels_ref, load_sem.at[7]),
        pltpu.make_async_copy(feats_hbm, feats_ref, load_sem.at[8]),
    ]
    for load in firsts + loads:
        load.start()
    for load in firsts:
        load.wait()

    ids = ids_ref[...]
    to_z = lax.rem(lax.div(ids, YS) - z + zs, zs)
    to_y = lax.rem(lax.rem(ids, YS) - y + YS, YS)
    spots = lax.rem(to_z * YS + to_y + turn, owners)
    member = iota((owners, tokens), 0) == spots
    member_b = member.astype(jnp.float32).astype(jnp.bfloat16)
    before = (iota((tokens, tokens), 0) < iota((tokens, tokens), 1)).astype(jnp.float32).astype(jnp.bfloat16)
    earlier = dot(member_b, before)
    rank = jnp.sum(jnp.where(member, earlier, 0.0), axis=0, keepdims=True).astype(jnp.int32)
    slot = spots * CAP + rank
    place = (iota((rows, tokens), 0) == slot).astype(jnp.float32).astype(jnp.bfloat16)
    out_x[...] = dot(place, feats_ref[...]).astype(jnp.bfloat16).reshape(owners, CAP, width)
    lane_t = iota((LANES, tokens), 0)
    labels_f = labels_ref[...].astype(jnp.float32)
    label_of = jnp.where(lax.rem(lane_t, 2) == 0, labels_f[0:1], labels_f[1:2])
    label_at = jnp.where(lax.div(lane_t, 2) == rank, label_of, 0.0).astype(jnp.bfloat16)
    lab_s[...] = dot(member_b, label_at, ((1,), (1,))).reshape(owners, 1, LANES)

    def send_x(group):
        def send(spot, target):
            pltpu.make_async_remote_copy(
                out_x.at[spot], x_ref.at[spot], x_send, x_recv.at[group], device_id=(grp, target), device_id_type=MESH
            ).start()

        return send

    def send_label(group):
        def send(spot, target):
            pltpu.make_async_remote_copy(
                lab_s.at[spot], lab_r.at[spot], lab_send, lab_recv.at[group], device_id=(grp, target), device_id_type=MESH
            ).start()

        return send

    greeted = near - 1
    pl.semaphore_wait(barrier, greeted + 1 + chips - 1)
    for end in (REACH, zs - REACH):
        pl.semaphore_signal(near_sem, inc=1, device_id=(grp, lax.rem(z + end, zs) * YS + y), device_id_type=MESH)
    near_rows(send_x(0))
    near_rows(send_label(0))
    pl.semaphore_wait(near_sem, 2)
    far_rows(send_x(1))
    far_rows(send_label(1))
    x_ref[turn] = out_x[turn]
    lab_r[turn] = lab_s[turn]

    def bulk(src, dst, count, send, recv):
        return pltpu.make_async_remote_copy(
            src.at[pl.ds(0, count)], dst.at[pl.ds(0, count)], send, recv, device_id=partner, device_id_type=MESH
        )

    for load in loads:
        load.wait()

    task_row = lax.div(iota((2 * LANES, 1), 0), LANES)
    gate_w = gate_ref[...].astype(jnp.float32)
    gate_b = jnp.where(task_row == 0, gate_w[0:1], gate_w[1:2]).astype(jnp.bfloat16)
    tout_w = tout_ref[...].astype(jnp.float32)
    tout = jnp.concatenate([tout_w[0:1], tout_w[1:2]], axis=1)
    same_task = lax.div(iota((2 * LANES, 2 * LANES), 0), LANES) == lax.div(iota((2 * LANES, 2 * LANES), 1), LANES)
    tout_b = jnp.where(same_task, tout, 0.0).astype(jnp.bfloat16)

    def own_lane(blocks):
        lane = iota((blocks * CAP, LANES), 1)
        return lane, lax.rem(iota((blocks * CAP, LANES), 0), CAP) == lax.div(lane, 2)

    def forward(first, blocks):
        x = x_ref[pl.ds(first, blocks)].reshape(blocks * CAP, width)
        block = blocks * CAP
        acc = None
        for c in range(CHUNKS):
            at = pl.ds(c * cols, cols)
            h = jnp.maximum(dot(x, w_ref[:, at]), 0.0).astype(jnp.bfloat16)
            s = jnp.maximum(dot(x, s_ref[:, at]), 0.0).astype(jnp.bfloat16)
            hidden[pl.ds(first * CAP, block), at] = h
            more = dot(jnp.concatenate([h, s], axis=0), t_ref[at, :])
            acc = more if acc is None else acc + more
        gate = jax.nn.sigmoid(dot(x, gate_b, ((1,), (1,))))
        tower_in = gate * acc[:block] + (1.0 - gate) * acc[block:]
        act = jnp.maximum(tower_in, 0.0).astype(jnp.bfloat16)
        logit = dot(act, tout_b, ((1,), (1,)))
        lane, mine = own_lane(blocks)
        pick = jnp.where(lax.rem(lane, 2) == 0, logit[:, :LANES], logit[:, LANES:])
        lg_s[pl.ds(first, blocks)] = jnp.sum(
            jnp.where(mine, pick, 0.0).reshape(blocks, CAP, LANES), axis=1, keepdims=True
        )
        return gate, tower_in, logit

    def send_logit(spot, target):
        pltpu.make_async_remote_copy(
            lg_s.at[spot], lg_r.at[spot], lg_send, lg_recv, device_id=(grp, target), device_id_type=MESH
        ).start()

    fan = (lax.rem(iota((LANES, 2 * LANES), 0), 2) == lax.div(iota((LANES, 2 * LANES), 1), LANES)).astype(jnp.float32).astype(jnp.bfloat16)
    weight = 64.0 / jnp.sqrt(jnp.full((1, 2 * LANES), counts_ref[own], jnp.int32).astype(jnp.float32))
    d_new = iota((width, width), 0)
    d_old = iota((width, width), 1)
    from_row = (2 * lax.rem(lax.div(d_new, part), chips) + lax.div(d_new, part * chips)) * part + lax.rem(d_new, part)
    order = (d_old == from_row).astype(jnp.float32).astype(jnp.bfloat16)

    def gradient(first, blocks, side):
        gate, tower_in, logit = side
        block = blocks * CAP
        spread = (lax.div(iota((block, blocks), 0), CAP) == iota((block, blocks), 1)).astype(jnp.float32).astype(jnp.bfloat16)
        packed = dot(spread, lab_r[pl.ds(first, blocks)].reshape(blocks, LANES).astype(jnp.bfloat16))
        packed = jnp.where(own_lane(blocks)[1], packed, 0.0).astype(jnp.bfloat16)
        dlogit = weight * (jax.nn.sigmoid(logit) - dot(packed, fan))
        mixed = jnp.where(tower_in > 0.0, gate * dlogit * tout, 0.0).astype(jnp.bfloat16)
        x = x_ref[pl.ds(first, blocks)].reshape(block, width)
        return mixed, dot(order, x, ((1,), (1,))).astype(jnp.bfloat16)

    def share(first, blocks, mixed, x_t, c):
        at = pl.ds(c * cols, cols)
        back = dot(mixed, t_ref[at, :], ((1,), (1,))).astype(jnp.bfloat16)
        masked = jnp.where(hidden[pl.ds(first * CAP, blocks * CAP), at] > 0.0, back, jnp.zeros_like(back))
        return dot(x_t, masked).reshape(2, width // 2, cols)

    def core_copy(c):
        return pltpu.make_async_remote_copy(
            core_s.at[c, 1 - core], core_r.at[c], core_send.at[c], core_recv.at[c], device_id=partner, device_id_type=MESH
        )

    def link_copy(c, d):
        to = lax.rem(chip + d, chips)
        return pltpu.make_async_remote_copy(
            link_s.at[c, to],
            link_r.at[c, d - 1],
            link_send.at[c, d - 1],
            link_recv.at[c, d - 1],
            device_id=(2 * to + core, own),
            device_id_type=MESH,
        )

    bulk(out_x, x_ref, near - 1, x_send, x_recv.at[0]).wait_recv()
    near_side = forward(0, near)
    near_rows(send_logit, back=True)
    lg_r[turn] = lg_s[turn]
    bulk(lab_s, lab_r, near - 1, lab_send, lab_recv.at[0]).wait_recv()
    mixed, x_t = gradient(0, near, near_side)
    for c in range(CHUNKS):
        core_f[c] = share(0, near, mixed, x_t, c)
    bulk(out_x, x_ref, far, x_send, x_recv.at[1]).wait_recv()
    far_side = forward(near, far)

    @pl.when(z >= early_z)
    def _():
        far_rows(send_logit, back=True)

    bulk(lab_s, lab_r, far, lab_send, lab_recv.at[1]).wait_recv()
    mixed, x_t = gradient(near, far, far_side)
    for c in range(CHUNKS):
        total = core_f[c] + share(near, far, mixed, x_t, c)
        core_f[c] = total
        core_s[c] = total.astype(jnp.bfloat16)
        core_copy(c).start()

    @pl.when(early)
    def _():
        far_rows(send_logit, back=True)

    for c in range(CHUNKS):
        core_copy(c).wait_recv()
        total = core_f[c, core] + core_r[c].astype(jnp.float32)
        proj[c] = total.reshape(chips, part, cols)
        link_s[c] = total.astype(jnp.bfloat16).reshape(chips, part, cols)
        for d in (2, 1, 3):
            link_copy(c, d).start()
    bulk(lg_s, lg_r, owners - 1, lg_send, lg_recv).wait_recv()
    got = lg_r[...].reshape(owners, LANES)
    found = dot(got, member.astype(jnp.float32), ((0,), (0,)), lax.Precision.HIGHEST)
    for task in range(2):
        logits_ref[pl.ds(task, 1), :] = jnp.sum(jnp.where(lane_t == 2 * rank + task, found, 0.0), axis=0, keepdims=True)

    for c in range(CHUNKS):
        total = proj[c, chip]
        for d in (1, 3, 2):
            link_copy(c, d).wait_recv()
            total = total + link_r[c, d - 1].astype(jnp.float32)
        grad_ref[0, :, pl.ds(c * cols, cols)] = total

    bulk(out_x, x_ref, owners - 1, x_send, x_recv.at[0]).wait_send()
    bulk(lab_s, lab_r, owners - 1, lab_send, lab_recv.at[0]).wait_send()
    bulk(lg_s, lg_r, owners - 1, lg_send, lg_recv).wait_send()
    for c in range(CHUNKS):
        core_copy(c).wait_send()
        for d in range(1, chips):
            link_copy(c, d).wait_send()


def shards(owners, groups, features, scenario_ids, labels, counts, scenario_weights, shared_weights, gate_weights, tower_weights, tower_out):
    tokens, width = features.shape
    expert, towers = tower_weights.shape
    cols = expert // CHUNKS
    part = width // groups
    chips = groups // 2
    vmem = pl.BlockSpec(memory_space=pltpu.VMEM)
    hbm = pl.BlockSpec(memory_space=pltpu.HBM)
    dma = pltpu.SemaphoreType.DMA
    bf16, f32 = jnp.bfloat16, jnp.float32
    return pl.pallas_call(
        functools.partial(step_kernel, owners, groups),
        out_shape=(pltpu.VMEM((2, tokens), f32), pltpu.VMEM((1, part, expert), f32)),
        in_specs=[hbm] * 9,
        out_specs=(vmem, vmem),
        scratch_shapes=[
            pltpu.VMEM((1, tokens), jnp.int32),
            pltpu.VMEM((2, tokens), jnp.int32),
            pltpu.VMEM((tokens, width), bf16),
            pltpu.SMEM((owners,), jnp.int32),
            pltpu.VMEM((2, width), bf16),
            pltpu.VMEM((2, towers // 2), bf16),
            pltpu.VMEM((width, expert), bf16),
            pltpu.VMEM((width, expert), bf16),
            pltpu.VMEM((expert, towers), bf16),
            pltpu.VMEM((owners, CAP, width), bf16),
            pltpu.VMEM((owners, CAP, width), bf16),
            pltpu.VMEM((owners, 1, LANES), f32),
            pltpu.VMEM((owners, 1, LANES), f32),
            pltpu.VMEM((owners, 1, LANES), f32),
            pltpu.VMEM((owners, 1, LANES), f32),
            pltpu.VMEM((owners * CAP, expert), bf16),
            pltpu.VMEM((CHUNKS, chips, part, cols), f32),
            pltpu.VMEM((CHUNKS, 2, width // 2, cols), bf16),
            pltpu.VMEM((CHUNKS, width // 2, cols), bf16),
            pltpu.VMEM((CHUNKS, 2, width // 2, cols), f32),
            pltpu.VMEM((CHUNKS, chips, part, cols), bf16),
            pltpu.VMEM((CHUNKS, chips - 1, part, cols), bf16),
            dma((9,)),
            dma(()),
            dma((2,)),
            dma(()),
            dma((2,)),
            dma(()),
            dma(()),
            pltpu.SemaphoreType.REGULAR,
            dma((CHUNKS,)),
            dma((CHUNKS,)),
            dma((CHUNKS, chips - 1)),
            dma((CHUNKS, chips - 1)),
        ],
        compiler_params=pltpu.CompilerParams(collective_id=0, has_side_effects=True, vmem_limit_bytes=56 * 1024 * 1024),
    )(
        scenario_ids.reshape(1, tokens),
        labels,
        features,
        counts,
        scenario_weights,
        shared_weights,
        gate_weights.T,
        tower_weights,
        tower_out.reshape(2, towers // 2),
    )


def solution(mesh):
    return jax.shard_map(
        functools.partial(shards, mesh.shape["own"], mesh.shape["grp"]),
        mesh=mesh,
        in_specs=(
            P(("grp", "own"), None),
            P(("grp", "own")),
            P(None, ("grp", "own")),
            P(),
            P("own", None, None),
            P(),
            P(),
            P(),
            P(),
        ),
        out_specs=(P(None, ("grp", "own")), P("own", "grp", None)),
        check_vma=False,
    )
```
